256 devices in a mesh: node: 16 (over x, z_hi), tm: 16 (over z_lo, y, core).
Axes of the slice: x: 4, y: 4, z: 8 (z_hi: 4, z_lo: 2; z = z_hi * 2 + z_lo), core: 2. Of those that a mesh axis runs over, the one named last changes fastest.
Arguments:
- codes: int32 [65536, 2048], P('node', 'tm'), may hold values from -127 to 127
- node_scale: float32 [65536], P('node'), may hold values from 0.002 to 0.02
- basis: bfloat16 [65536, 128], P('node'), may hold values from -0.0234375 to 0.0234375
- regular: float32 [8384], replicated, may hold values from 0.05 to 0.5
- feature_order: int32 [8384], replicated, may hold values from 0 to 8383, each once
- panel_inverse: float32 [2, 262, 262], replicated, may hold values from -0.06 to 1.2
Outputs:
- schur: float32 [8384, 8384], P('node', 'tm')
The draws below stay inside these ranges and needn't reach their ends.
Inputs may be any that keep to these rules, and one draw needn't show every extreme that they name: `feature_order`: a permutation: every feature stands at exactly one position.
All inputs are finite; a program needn't handle non-finite values.
Results may differ from the reference program's by a relative error of at most 0.0051.
Values sent between devices are 32-bit elements; how exact they have to be, the bound alone decides.
A program may use at most 64 MiB of HBM per device.

```python
import math
import jax
import jax.numpy as jnp
import numpy as np
from jax import lax

RANK = 128
PW = 262
PANELS = 2
NODE_DEV = 4096
NFEAT = 8384
NODES = 65536
SNAPS = 2048
N_NODE = 16


def draw_panel_inverse(key, part):
    key_off = jax.random.fold_in(key, 11)
    key_diag = jax.random.fold_in(key, 12)
    offdiag = jnp.clip(0.045 * jax.random.normal(key_off, (PANELS, PW, PW), jnp.float32), -0.06, 0.06)
    diagonal = 0.6 + 0.6 * jax.random.uniform(key_diag, (PANELS, PW), jnp.float32)
    symmetric = 0.5 * (offdiag + jnp.swapaxes(offdiag, 1, 2))
    identity = jnp.eye(PW, dtype=jnp.float32)
    return symmetric * (1.0 - identity) + diagonal[:, :, None] * identity


def plant(result, own_key, smallest, largest):
    longest = result.shape.index(max(result.shape))
    spots = []
    for shift in (0, 1):
        where = [jax.random.randint(jax.random.fold_in(own_key, axis), (), 0, length) for axis, length in enumerate(result.shape)]
        where[longest] = (where[longest] + shift) % result.shape[longest]
        spots.append(tuple(where))
    return result.at[spots[0]].set(smallest).at[spots[1]].set(largest)


def shard_levels(own_key, extent, cuts, least, high):
    level, own = 1.0, jax.random.fold_in(own_key, 6)
    for position, blocks in cuts:
        heights = jnp.exp(jax.random.uniform(jax.random.fold_in(own, position), (blocks,), jnp.float32, least / len(cuts), high / len(cuts)))
        level = level * jnp.repeat(heights, extent[position] // blocks).reshape([-1 if axis == position else 1 for axis in range(len(extent))])
    return level


def gaussian(own_key, extent, scale, bound, split=(), held_as=jnp.bfloat16):
    drawn = scale * jax.random.normal(own_key, extent, jnp.float32)
    if split:
        drawn = drawn * shard_levels(own_key, extent, split, -0.22, 0.18)
    return jnp.clip(drawn, -bound, bound).astype(held_as)


def setup_inputs(seed: int = 0) -> dict:
    splits = jax.random.split(jax.random.key(seed), 7)
    codes = plant(jax.random.randint(splits[0], (NODES, SNAPS), -127, 128), jax.random.fold_in(splits[0], 1), -127, 127).astype(jnp.int32)
    node_scale = jnp.clip(jnp.exp(math.log(0.02) - 2.30258502 * jax.random.uniform(splits[1], (NODES,), jnp.float32) ** shard_levels(splits[1], (NODES,), ((0, 16),), -0.2, 0.2)), 0.002, 0.02)
    basis = gaussian(splits[2], (NODES, RANK), NODES ** -0.5, 0.0234375, ((0, 16),))
    regular = jnp.clip(jnp.exp(jax.random.uniform(splits[3], (NFEAT,), jnp.float32, math.log(0.05), math.log(0.5))), 0.05, 0.5)
    feature_order = jax.random.permutation(splits[4], NFEAT).astype(jnp.int32)
    panel_inverse = draw_panel_inverse(jax.random.fold_in(splits[6], 71), 0)
    return dict(codes=codes, node_scale=node_scale, basis=basis, regular=regular, feature_order=feature_order, panel_inverse=panel_inverse)


def pair_tables(rank_count):
    former_list = []
    latter_list = []
    for leading in range(rank_count + 1):
        for trailing in range(leading, rank_count + 1):
            if leading < rank_count or trailing < rank_count:
                former_list.append(leading)
                latter_list.append(trailing)
    return np.array(former_list, np.int32), np.array(latter_list, np.int32)


def reference(codes, node_scale, basis, regular, feature_order, panel_inverse):
    scaled_basis = (basis.astype(jnp.float32) * node_scale[:, None]).astype(jnp.bfloat16)
    code_blocks = codes.reshape(N_NODE, NODE_DEV, SNAPS)
    basis_blocks = scaled_basis.reshape(N_NODE, NODE_DEV, RANK)

    def project(running, blocks):
        code_block, basis_block = blocks
        added = lax.dot_general(code_block.astype(jnp.bfloat16), basis_block, (((0,), (0,)), ((), ())), preferred_element_type=jnp.float32)
        return running + added, None

    trajectories, _ = lax.scan(project, jnp.zeros((SNAPS, RANK), jnp.float32), (code_blocks, basis_blocks))
    former, latter = pair_tables(RANK)
    extended = jnp.concatenate([trajectories, jnp.ones((SNAPS, 1), jnp.float32)], axis=1)
    leading = jnp.take(jnp.asarray(former), feature_order)
    trailing = jnp.take(jnp.asarray(latter), feature_order)
    features = (jnp.take(extended, leading, axis=1) * jnp.take(extended, trailing, axis=1)).astype(jnp.bfloat16)
    gram = lax.dot_general(features, features, (((0,), (0,)), ((), ())), preferred_element_type=jnp.float32) / SNAPS
    matrix = gram + jnp.diag(regular)
    for panel in range(PANELS):
        lower = panel * PW
        left_part = matrix[:, lower:lower + PW]
        upper_part = matrix[lower:lower + PW, :]
        scaled_left = jnp.dot(left_part, panel_inverse[panel], precision=lax.Precision.HIGHEST, preferred_element_type=jnp.float32)
        matrix = matrix - jnp.dot(scaled_left, upper_part, precision=lax.Precision.HIGHEST, preferred_element_type=jnp.float32)
    return matrix
```

```python
import jax
import jax.numpy as jnp
import numpy as np
from jax import lax
from jax.sharding import PartitionSpec as P


def pair_starts(rank_count):
    leading = np.arange(rank_count + 1)
    return (leading * (rank_count + 1) - leading * (leading - 1) // 2).astype(np.int32)


def selectors(chosen, rank_count):
    starts = pair_starts(rank_count)
    modes = jnp.arange(rank_count, dtype=jnp.int32)
    below = chosen[:, None] >= jnp.asarray(starts[:-1])[None, :]
    above = chosen[:, None] < jnp.asarray(starts[1:])[None, :]
    lead = jnp.logical_and(below, above)
    shift = modes - jnp.asarray(starts[:-1])
    trailing = chosen + jnp.sum(jnp.where(lead, shift[None, :], 0), axis=1)
    trail = trailing[:, None] == modes[None, :]
    keep = (trailing < rank_count).astype(jnp.float32)
    return lead.astype(jnp.bfloat16), trail.astype(jnp.bfloat16), 1.0 - keep


def spread(values):
    high = lax.reduce_precision(values, 8, 7)
    low = lax.reduce_precision(values - high, 8, 7)
    return jnp.concatenate([high, low], axis=1).astype(jnp.bfloat16)


def make_features(pieces, picks):
    lead, trail, constant = picks
    dims = (((1,), (1,)), ((), ()))
    lead = jnp.concatenate([lead, lead], axis=1)
    trail = jnp.concatenate([trail, trail], axis=1)
    lead_vals = lax.dot_general(lead, pieces, dims, preferred_element_type=jnp.float32)
    trail_vals = lax.dot_general(trail, pieces, dims, preferred_element_type=jnp.float32)
    return (lead_vals * (trail_vals + constant[:, None])).astype(jnp.bfloat16)


def contract(left_feats, right_feats):
    return lax.dot_general(
        left_feats, right_feats, (((1,), (1,)), ((), ())), preferred_element_type=jnp.float32
    )


def highest(left_mat, right_mat):
    return jnp.dot(
        left_mat, right_mat, precision=lax.Precision.HIGHEST, preferred_element_type=jnp.float32
    )


def per_device(codes, node_scale, basis, regular, feature_order, panel_inverse):
    rank_count = basis.shape[1]
    snap_local = codes.shape[1]
    nfeat = regular.shape[0]
    row_size = nfeat // lax.axis_size("node")
    col_size = nfeat // lax.axis_size("tm")
    snap_total = snap_local * lax.axis_size("tm")
    panel_width = panel_inverse.shape[1]
    span = 2 * panel_width
    scaled_basis = (basis.astype(jnp.float32) * node_scale[:, None]).astype(jnp.bfloat16)
    code_values = codes.astype(jnp.bfloat16)
    row_offset = lax.axis_index("node") * row_size
    col_offset = lax.axis_index("tm") * col_size
    row_picks = selectors(lax.dynamic_slice_in_dim(feature_order, row_offset, row_size), rank_count)
    col_picks = selectors(lax.dynamic_slice_in_dim(feature_order, col_offset, col_size), rank_count)
    pan_picks = selectors(feature_order[:span], rank_count)
    summed = lax.psum(
        lax.dot_general(
            code_values, scaled_basis, (((0,), (0,)), ((), ())), preferred_element_type=jnp.float32
        ),
        "node",
    )
    pieces = spread(lax.all_gather(summed, "tm", axis=0, tiled=True))
    row_feats = make_features(pieces, row_picks)
    col_feats = make_features(pieces, col_picks)
    pan_feats = make_features(pieces, pan_picks)
    row_global = row_offset + jnp.arange(row_size, dtype=jnp.int32)
    col_global = col_offset + jnp.arange(col_size, dtype=jnp.int32)
    pan_global = jnp.arange(span, dtype=jnp.int32)
    row_regular = lax.dynamic_slice_in_dim(regular, row_offset, row_size)

    def block(left_feats, right_feats, left_global, right_global, left_regular):
        same = (left_global[:, None] == right_global[None, :]).astype(jnp.float32)
        return contract(left_feats, right_feats) / snap_total + same * left_regular[:, None]

    matrix = block(row_feats, col_feats, row_global, col_global, row_regular)
    left = block(row_feats, pan_feats, row_global, pan_global, row_regular)
    upper = block(pan_feats, col_feats, pan_global, col_global, regular[:span])
    w = panel_width
    inner = contract(pan_feats[:w], pan_feats[w:]) / snap_total
    first_left = highest(left[:, :w], panel_inverse[0])
    second_left = left[:, w:] - highest(first_left, inner)
    cross = highest(panel_inverse[0], inner)
    second_upper = upper[w:] - highest(cross.T, upper[:w])
    second_left = highest(second_left, panel_inverse[1])
    joint = jnp.concatenate([first_left, second_left], axis=1)
    return matrix - highest(joint, jnp.concatenate([upper[:w], second_upper], axis=0))


def solution(mesh):
    placed = (P("node", "tm"), P("node"), P("node", None), P(), P(), P())
    return jax.shard_map(
        per_device, mesh=mesh, in_specs=placed, out_specs=P("node", "tm"), check_vma=False
    )
```

```python
import jax
import jax.numpy as jnp
import numpy as np
from jax import lax
from jax.experimental import pallas as pl
from jax.experimental.pallas import tpu as pltpu
from jax.sharding import PartitionSpec as P

MESH = pl.DeviceIdType.MESH


def pair_starts(rank_count):
    leading = np.arange(rank_count + 1)
    return (leading * (rank_count + 1) - leading * (leading - 1) // 2).astype(np.int32)


def selectors(chosen, rank_count):
    starts = pair_starts(rank_count)
    modes = jnp.arange(rank_count, dtype=jnp.int32)
    below = chosen[:, None] >= jnp.asarray(starts[:-1])[None, :]
    above = chosen[:, None] < jnp.asarray(starts[1:])[None, :]
    lead = jnp.logical_and(below, above)
    shift = modes - jnp.asarray(starts[:-1])
    trailing = chosen + jnp.sum(jnp.where(lead, shift[None, :], 0), axis=1)
    trail = trailing[:, None] == modes[None, :]
    keep = (trailing < rank_count).astype(jnp.float32)
    return lead.astype(jnp.bfloat16), trail.astype(jnp.bfloat16), 1.0 - keep


def spread(values):
    high = lax.reduce_precision(values, 8, 7)
    low = lax.reduce_precision(values - high, 8, 7)
    return jnp.concatenate([high, low], axis=1).astype(jnp.bfloat16)


def make_features(pieces, picks):
    lead, trail, constant = picks
    dims = (((1,), (1,)), ((), ()))
    lead = jnp.concatenate([lead, lead], axis=1)
    trail = jnp.concatenate([trail, trail], axis=1)
    lead_vals = lax.dot_general(lead, pieces, dims, preferred_element_type=jnp.float32)
    trail_vals = lax.dot_general(trail, pieces, dims, preferred_element_type=jnp.float32)
    return (lead_vals * (trail_vals + constant[:, None])).astype(jnp.bfloat16)


def contract(left_feats, right_feats):
    return lax.dot_general(
        left_feats, right_feats, (((1,), (1,)), ((), ())), preferred_element_type=jnp.float32
    )


def highest(left_mat, right_mat):
    return jnp.dot(
        left_mat, right_mat, precision=lax.Precision.HIGHEST, preferred_element_type=jnp.float32
    )


def gather_kernel(
    scale_ref, codes_hbm, basis_hbm, out_ref,
    codes_buf, basis_buf, total, partial, slots,
    code_sem, basis_sem, rs_send, rs_recv, z_send, z_recv, xy_send, xy_recv, sib_send, sib_recv,
):
    node, tm = lax.axis_index("node"), lax.axis_index("tm")
    x, z_hi = lax.div(node, 4), lax.rem(node, 4)
    z_lo, y, core = lax.div(tm, 8), lax.rem(lax.div(tm, 2), 4), lax.rem(tm, 2)
    z = z_hi * 2 + z_lo

    def place(at_x, at_y, at_z, at_core):
        return (at_x * 4 + lax.div(at_z, 2), lax.rem(at_z, 2) * 8 + at_y * 2 + at_core)

    def node_peer(step):
        return (lax.rem(node + step, 16), tm)

    def z_peer(step):
        return place(x, y, lax.rem(z + step, 8), core)

    def xy_peer(step):
        return place(lax.rem(x + lax.div(step, 4), 4), lax.rem(y + lax.rem(step, 4), 4), z, core)

    sibling = place(x, y, z, 1 - core)

    chunks = code_sem.shape[0]
    rows = codes_buf.shape[0] // chunks
    for chunk in range(chunks):
        part = pl.ds(chunk * rows, rows)
        pltpu.make_async_copy(codes_hbm.at[part], codes_buf.at[part], code_sem.at[chunk]).start()
        pltpu.make_async_copy(basis_hbm.at[part], basis_buf.at[part], basis_sem.at[chunk]).start()

    barrier = pltpu.get_barrier_semaphore()

    def greet(peer):
        pl.semaphore_signal(barrier, inc=1, device_id=peer, device_id_type=MESH)

    @pl.loop(1, 16)
    def _(step):
        greet(node_peer(step))
        greet(xy_peer(step))

    @pl.loop(1, 8)
    def _(step):
        greet(z_peer(step))

    greet(sibling)

    total[...] = jnp.zeros_like(total)
    for chunk in range(chunks):
        part = pl.ds(chunk * rows, rows)
        pltpu.make_async_copy(codes_hbm.at[part], codes_buf.at[part], code_sem.at[chunk]).wait()
        pltpu.make_async_copy(basis_hbm.at[part], basis_buf.at[part], basis_sem.at[chunk]).wait()
        turned = []
        for piece in range(rows // 128):
            row = chunk * (rows // 128) + piece
            basis = basis_buf[pl.ds(row * 128, 128), :].astype(jnp.float32)
            turned.append((basis.T * scale_ref[row : row + 1, :]).astype(jnp.bfloat16))
        turned = jnp.concatenate(turned, axis=1)
        values = codes_buf[part, :].astype(jnp.float32).astype(jnp.bfloat16)
        total[...] += jnp.dot(turned, values, preferred_element_type=jnp.float32)
    partial[...] = total[...].T.reshape(partial.shape)

    pl.semaphore_wait(barrier, 38)

    def rs_copy(step):
        peer = node_peer(step)
        return pltpu.make_async_remote_copy(
            src_ref=partial.at[peer[0]], dst_ref=slots.at[step],
            send_sem=rs_send.at[step], recv_sem=rs_recv.at[step],
            device_id=peer, device_id_type=MESH,
        )

    block = (x * 4 + y) * 2 + core

    def z_copy(step):
        return pltpu.make_async_remote_copy(
            src_ref=out_ref.at[block * 8 + z], dst_ref=out_ref.at[block * 8 + z],
            send_sem=z_send.at[step], recv_sem=z_recv.at[step],
            device_id=z_peer(step), device_id_type=MESH,
        )

    def xy_copy(step):
        part = pl.ds(block * 8, 8)
        return pltpu.make_async_remote_copy(
            src_ref=out_ref.at[part], dst_ref=out_ref.at[part],
            send_sem=xy_send.at[step], recv_sem=xy_recv.at[step],
            device_id=xy_peer(step), device_id_type=MESH,
        )

    def sib_copy(step):
        from_x = lax.rem(x + 4 - lax.div(step, 4), 4)
        from_y = lax.rem(y + 4 - lax.rem(step, 4), 4)
        part = pl.ds(((from_x * 4 + from_y) * 2 + core) * 8, 8)
        return pltpu.make_async_remote_copy(
            src_ref=out_ref.at[part], dst_ref=out_ref.at[part],
            send_sem=sib_send.at[step], recv_sem=sib_recv.at[step],
            device_id=sibling, device_id_type=MESH,
        )

    @pl.loop(1, 16)
    def _(step):
        rs_copy(step).start()

    @pl.loop(1, 16)
    def _(step):
        rs_copy(step).wait_recv()

    summed = partial[node]
    for step in range(1, 16):
        summed = summed + slots[step]
    out_ref[block * 8 + z] = summed

    @pl.loop(1, 8)
    def _(step):
        z_copy(step).start()

    @pl.loop(1, 8)
    def _(step):
        z_copy(step).wait_recv()

    @pl.loop(1, 16)
    def _(step):
        xy_copy(step).start()

    sib_copy(0).start()

    @pl.loop(1, 16)
    def _(step):
        xy_copy(step).wait_recv()
        sib_copy(step).start()

    @pl.loop(0, 16)
    def _(step):
        sib_copy(step).wait_recv()

    sib_copy(0).wait_send()

    @pl.loop(1, 16)
    def _(step):
        rs_copy(step).wait_send()
        xy_copy(step).wait_send()
        sib_copy(step).wait_send()

    @pl.loop(1, 8)
    def _(step):
        z_copy(step).wait_send()


def gathered(codes, node_scale, basis):
    nodes, snaps = codes.shape
    modes = basis.shape[1]
    chunks = 8
    dma = pltpu.SemaphoreType.DMA
    out = pl.pallas_call(
        gather_kernel,
        out_shape=jax.ShapeDtypeStruct((256, 8, modes), jnp.float32),
        in_specs=[
            pl.BlockSpec(memory_space=pltpu.VMEM),
            pl.BlockSpec(memory_space=pl.ANY),
            pl.BlockSpec(memory_space=pl.ANY),
        ],
        out_specs=pl.BlockSpec(memory_space=pltpu.VMEM),
        scratch_shapes=[
            pltpu.VMEM((nodes, snaps), jnp.int32),
            pltpu.VMEM((nodes, modes), jnp.bfloat16),
            pltpu.VMEM((modes, snaps), jnp.float32),
            pltpu.VMEM((16, 8, modes), jnp.float32),
            pltpu.VMEM((16, 8, modes), jnp.float32),
            dma((chunks,)), dma((chunks,)),
            dma((16,)), dma((16,)), dma((8,)), dma((8,)), dma((16,)), dma((16,)), dma((16,)), dma((16,)),
        ],
        compiler_params=pltpu.CompilerParams(
            collective_id=0, has_side_effects=True, vmem_limit_bytes=32 * 1024 * 1024
        ),
        name="project_and_gather",
    )(node_scale.reshape(nodes // 128, 128), codes, basis)
    return out.reshape(256 * 8, modes)


def per_device(codes, node_scale, basis, regular, feature_order, panel_inverse):
    rank_count = basis.shape[1]
    snap_local = codes.shape[1]
    nfeat = regular.shape[0]
    row_size = nfeat // lax.axis_size("node")
    col_size = nfeat // lax.axis_size("tm")
    snap_total = snap_local * lax.axis_size("tm")
    panel_width = panel_inverse.shape[1]
    span = 2 * panel_width
    row_offset = lax.axis_index("node") * row_size
    col_offset = lax.axis_index("tm") * col_size
    row_picks = selectors(lax.dynamic_slice_in_dim(feature_order, row_offset, row_size), rank_count)
    col_picks = selectors(lax.dynamic_slice_in_dim(feature_order, col_offset, col_size), rank_count)
    pan_picks = selectors(feature_order[:span], rank_count)
    pieces = spread(gathered(codes, node_scale, basis))
    row_feats = make_features(pieces, row_picks)
    col_feats = make_features(pieces, col_picks)
    pan_feats = make_features(pieces, pan_picks)
    row_global = row_offset + jnp.arange(row_size, dtype=jnp.int32)
    col_global = col_offset + jnp.arange(col_size, dtype=jnp.int32)
    pan_global = jnp.arange(span, dtype=jnp.int32)
    row_regular = lax.dynamic_slice_in_dim(regular, row_offset, row_size)

    def block(left_feats, right_feats, left_global, right_global, left_regular):
        same = (left_global[:, None] == right_global[None, :]).astype(jnp.float32)
        return contract(left_feats, right_feats) / snap_total + same * left_regular[:, None]

    matrix = block(row_feats, col_feats, row_global, col_global, row_regular)
    left = block(row_feats, pan_feats, row_global, pan_global, row_regular)
    upper = block(pan_feats, col_feats, pan_global, col_global, regular[:span])
    w = panel_width
    inner = contract(pan_feats[:w], pan_feats[w:]) / snap_total
    first_left = highest(left[:, :w], panel_inverse[0])
    second_left = left[:, w:] - highest(first_left, inner)
    cross = highest(panel_inverse[0], inner)
    second_upper = upper[w:] - highest(cross.T, upper[:w])
    second_left = highest(second_left, panel_inverse[1])
    joint = jnp.concatenate([first_left, second_left], axis=1)
    return matrix - highest(joint, jnp.concatenate([upper[:w], second_upper], axis=0))


def solution(mesh):
    placed = (P("node", "tm"), P("node"), P("node", None), P(), P(), P())
    return jax.shard_map(
        per_device, mesh=mesh, in_specs=placed, out_specs=P("node", "tm"), check_vma=False
    )
```

```python
import jax
import jax.numpy as jnp
from jax import lax
from jax.experimental import pallas as pl
from jax.experimental.pallas import tpu as pltpu
from jax.sharding import PartitionSpec as P

MESH = pl.DeviceIdType.MESH
F32, BF16 = jnp.float32, jnp.bfloat16
ROWS = 528
COLS = 640
WIDE = 384
TALL = 272
COL_AT, FIRST_AT, SECOND_AT = COLS, 2 * COLS, 2 * COLS + WIDE
ALL = 2 * COLS + 2 * WIDE


def nt(left, right):
    return lax.dot_general(left, right, (((1,), (1,)), ((), ())), preferred_element_type=F32)


def nn(left, right):
    return lax.dot_general(left, right, (((1,), (0,)), ((), ())), preferred_element_type=F32)


def halves(values):
    high = values.astype(BF16)
    return high, (values - high.astype(F32)).astype(BF16)


def thrice(dot, left, right):
    return dot(left[0], right[0]) + dot(left[0], right[1]) + dot(left[1], right[0])


def kernel(
    order_ref, regular_ref, scale_ref, panel_ref, codes_hbm, basis_hbm, out_ref,
    codes_buf, basis_buf, partial, slots, table, lead, trail, constant, feats,
    row_acc, first_acc, second_acc, cross_acc, inv_high, inv_low,
    code_sem, basis_sem, rs_send, rs_recv, z_send, z_recv, xy_send, xy_recv, sib_send, sib_recv,
):
    node, tm = lax.axis_index("node"), lax.axis_index("tm")
    x, z_hi = node // 4, node % 4
    z_lo, y, core = tm // 8, (tm // 2) % 4, tm % 2
    z = z_hi * 2 + z_lo
    modes = basis_buf.shape[1]
    width = panel_ref.shape[0]
    size = out_ref.shape[0]

    def place(at_x, at_y, at_z, at_core):
        return (at_x * 4 + at_z // 2, (at_z % 2) * 8 + at_y * 2 + at_core)

    def node_peer(step):
        return ((node + step) % 16, tm)

    def z_peer(step):
        return place(x, y, (z + step) % 8, core)

    def xy_peer(step):
        return place((x + step // 4) % 4, (y + step % 4) % 4, z, core)

    sibling = place(x, y, z, 1 - core)
    block = (x * 4 + y) * 2 + core

    def rs_copy(step):
        peer = node_peer(step)
        return pltpu.make_async_remote_copy(
            src_ref=partial.at[peer[0]], dst_ref=slots.at[step],
            send_sem=rs_send.at[step], recv_sem=rs_recv.at[step],
            device_id=peer, device_id_type=MESH,
        )

    def z_copy(step):
        piece = table.at[block, pl.ds(z * 8, 8)]
        return pltpu.make_async_remote_copy(
            src_ref=piece, dst_ref=piece, send_sem=z_send.at[step], recv_sem=z_recv.at[step],
            device_id=z_peer(step), device_id_type=MESH,
        )

    def xy_copy(step):
        return pltpu.make_async_remote_copy(
            src_ref=table.at[block], dst_ref=table.at[block],
            send_sem=xy_send.at[step], recv_sem=xy_recv.at[step],
            device_id=xy_peer(step), device_id_type=MESH,
        )

    def sib_copy(step):
        from_x, from_y = (x + 4 - step // 4) % 4, (y + 4 - step % 4) % 4
        at = (from_x * 4 + from_y) * 2 + core
        return pltpu.make_async_remote_copy(
            src_ref=table.at[at], dst_ref=table.at[at],
            send_sem=sib_send.at[step], recv_sem=sib_recv.at[step],
            device_id=sibling, device_id_type=MESH,
        )

    chunks = code_sem.shape[0]
    rows = codes_buf.shape[0] // chunks

    def fetch(chunk):
        part = pl.ds(chunk * rows, rows)
        return (
            pltpu.make_async_copy(codes_hbm.at[part], codes_buf.at[part], code_sem.at[chunk]),
            pltpu.make_async_copy(basis_hbm.at[part], basis_buf.at[part], basis_sem.at[chunk]),
        )

    for chunk in range(chunks):
        for copy in fetch(chunk):
            copy.start()

    barrier = pltpu.get_barrier_semaphore()

    def greet(peer):
        pl.semaphore_signal(barrier, inc=1, device_id=peer, device_id_type=MESH)

    @pl.loop(1, 16)
    def _(step):
        greet(node_peer(step))
        greet(xy_peer(step))

    @pl.loop(1, 8)
    def _(step):
        greet(z_peer(step))

    greet(sibling)

    total = jnp.zeros((modes, codes_buf.shape[1]), F32)
    for chunk in range(chunks):
        for copy in fetch(chunk):
            copy.wait()
        turned = []
        for piece in range(rows // 128):
            row = chunk * (rows // 128) + piece
            basis = basis_buf[pl.ds(row * 128, 128), :].astype(F32)
            turned.append((basis.T * scale_ref[row : row + 1, :]).astype(BF16))
        values = codes_buf[pl.ds(chunk * rows, rows), :].astype(F32).astype(BF16)
        total = total + nn(jnp.concatenate(turned, axis=1), values)
    partial[...] = total.T.reshape(partial.shape)

    pl.semaphore_wait(barrier, 38)

    @pl.loop(1, 16)
    def _(step):
        rs_copy(step).start()

    mode = lax.broadcasted_iota(jnp.int32, (128, 128), 1)
    start = mode * (modes + 1) - mode * (mode - 1) // 2

    @pl.loop(0, ALL // 128)
    def _(at):
        chosen = jnp.broadcast_to(order_ref[pl.ds(at, 1), :], (128, 128)).T.astype(jnp.int32)
        among = jnp.logical_and(chosen >= start, chosen < start + (modes + 1 - mode))
        shift = jnp.sum(jnp.where(among, (mode - start).astype(F32), 0.0), axis=1, keepdims=True)
        trailing = chosen + jnp.broadcast_to(shift, (128, 128)).astype(jnp.int32)
        part = pl.ds(at * 128, 128)
        among = jnp.where(among, 1.0, 0.0).astype(BF16)
        lead[part, 0:128] = among
        lead[part, 128:256] = among
        same = jnp.where(trailing == mode, 1.0, 0.0).astype(BF16)
        trail[part, 0:128] = same
        trail[part, 128:256] = same
        constant[part, :] = jnp.where(trailing == modes, 1.0, 0.0)

    feats[...] = jnp.zeros_like(feats)
    row_acc[...] = jnp.zeros_like(row_acc)
    first_acc[...] = jnp.zeros_like(first_acc)
    second_acc[...] = jnp.zeros_like(second_acc)
    cross_acc[...] = jnp.zeros_like(cross_acc)
    inv_high[...] = jnp.zeros_like(inv_high)
    inv_low[...] = jnp.zeros_like(inv_low)
    for panel in range(2):
        high, low = halves(panel_ref[:, panel, :])
        inv_high[panel, 0:width, 0:width] = high
        inv_low[panel, 0:width, 0:width] = low

    @pl.loop(1, 16)
    def _(step):
        rs_copy(step).wait_recv()

    summed = partial[node]
    for step in range(1, 16):
        summed = summed + slots[step]
    table[block, pl.ds(z * 8, 8), :] = summed

    @pl.loop(1, 8)
    def _(step):
        z_copy(step).start()

    @pl.loop(1, 8)
    def _(step):
        z_copy(step).wait_recv()

    for step in (1, 3, 2, 4, 5, 7, 6, 12, 13, 15, 14, 8, 9, 11, 10):
        xy_copy(step).start()
    sib_copy(0).start()
    for step in (1, 3, 2):
        xy_copy(step).wait_recv()
        sib_copy(step).start()
    for step in range(4):
        sib_copy(step).wait_recv()

    for turn, plane in enumerate((0, 1, 3, 2)):
        snaps = 8 * table.shape[1]
        values = table[pl.ds(((x + 4 - plane) % 4) * 8, 8)].reshape(snaps, modes)
        pieces = jnp.concatenate(halves(values), axis=1)
        for low, count in ((0, ROWS), (COL_AT, ROWS), (FIRST_AT, TALL), (SECOND_AT, TALL)):
            part = slice(low, low + count)
            once = jnp.concatenate([constant[part, :]] * (snaps // 128), axis=1)
            product = nt(lead[part, :], pieces) * (nt(trail[part, :], pieces) + once)
            feats[part, :] = product.astype(BF16)
        if turn < 3:
            after = (0, 1, 3, 2)[turn + 1]
            for step in (0, 1, 3, 2):
                xy_copy(after * 4 + step).wait_recv()
                sib_copy(after * 4 + step).start()
        columns = feats[COL_AT:FIRST_AT, :]
        row_acc[...] += nt(feats[0:ROWS, :], feats[COL_AT:ALL, :])
        first_acc[0:TALL, :] += nt(feats[FIRST_AT : FIRST_AT + TALL, :], columns)
        second = feats[SECOND_AT : SECOND_AT + TALL, :]
        second_acc[0:TALL, :] += nt(second, columns)
        cross_acc[0:TALL, :] += nt(second, feats[FIRST_AT:SECOND_AT, :])
        if turn < 3:
            for step in range(4):
                sib_copy(after * 4 + step).wait_recv()

    sib_copy(0).wait_send()

    @pl.loop(1, 16)
    def _(step):
        rs_copy(step).wait_send()
        xy_copy(step).wait_send()
        sib_copy(step).wait_send()

    @pl.loop(1, 8)
    def _(step):
        z_copy(step).wait_send()

    share = 1.0 / (table.shape[0] * table.shape[1])

    def diagonal(row_from, col_from, height, length, at):
        row = lax.broadcasted_iota(jnp.int32, (height, length), 0) + row_from
        col = lax.broadcasted_iota(jnp.int32, (height, length), 1) + col_from
        return jnp.where(row == col, regular_ref[0:1, at : at + length], 0.0)

    row_from, col_from = node * size, tm * size
    first_left = row_acc[:, COLS : COLS + WIDE] * share + diagonal(row_from, 0, ROWS, WIDE, COLS)
    second_left = row_acc[:, COLS + WIDE :] * share + diagonal(row_from, width, ROWS, WIDE, COLS + WIDE)
    first_up = halves(first_acc[...] * share + diagonal(0, col_from, WIDE, COLS, 0))
    second_up = second_acc[...] * share + diagonal(width, col_from, WIDE, COLS, 0)
    cross = halves(cross_acc[...] * share)
    first_inv = (inv_high[0], inv_low[0])
    second_inv = (inv_high[1], inv_low[1])
    first_left = halves(thrice(nn, halves(first_left), first_inv))
    second_left = second_left - thrice(nt, first_left, cross)
    second_left = halves(thrice(nn, halves(second_left), second_inv))
    second_up = halves(second_up - thrice(nn, halves(thrice(nn, cross, first_inv)), first_up))
    result = row_acc[:, 0:COLS] * share + diagonal(row_from, col_from, ROWS, COLS, 0)
    result = result - thrice(nn, first_left, first_up) - thrice(nn, second_left, second_up)
    out_ref[...] = result[0:size, 0:size]


def per_device(codes, node_scale, basis, regular, feature_order, panel_inverse):
    nodes, snaps = codes.shape
    modes = basis.shape[1]
    size = regular.shape[0] // lax.axis_size("node")
    width = panel_inverse.shape[1]
    row_from, col_from = lax.axis_index("node") * size, lax.axis_index("tm") * size

    def pick(values, low, count, length, fill):
        taken = lax.dynamic_slice_in_dim(values, low, count)
        return jnp.pad(taken, (0, length - count), constant_values=fill)

    order = feature_order.astype(F32)
    order = jnp.concatenate([
        pick(order, row_from, size, COLS, -1.0), pick(order, col_from, size, COLS, -1.0),
        pick(order, 0, width, WIDE, -1.0), pick(order, width, width, WIDE, -1.0),
    ]).reshape(ALL // 128, 128)
    diagonal = jnp.concatenate([
        pick(regular, col_from, size, COLS, 0.0),
        pick(regular, 0, width, WIDE, 0.0), pick(regular, width, width, WIDE, 0.0),
    ]).reshape(1, COLS + 2 * WIDE)
    chunks = 8
    dma = pltpu.SemaphoreType.DMA
    vmem = pl.BlockSpec(memory_space=pltpu.VMEM)
    hbm = pl.BlockSpec(memory_space=pltpu.HBM)
    return pl.pallas_call(
        kernel,
        out_shape=jax.ShapeDtypeStruct((size, size), F32),
        in_specs=[vmem, vmem, vmem, vmem, hbm, hbm],
        out_specs=vmem,
        scratch_shapes=[
            pltpu.VMEM((nodes, snaps), jnp.int32),
            pltpu.VMEM((nodes, modes), BF16),
            pltpu.VMEM((16, 8, modes), F32),
            pltpu.VMEM((16, 8, modes), F32),
            pltpu.VMEM((32, 64, modes), F32),
            pltpu.VMEM((ALL, 2 * modes), BF16),
            pltpu.VMEM((ALL, 2 * modes), BF16),
            pltpu.VMEM((ALL, 128), F32),
            pltpu.VMEM((ALL, 512), BF16),
            pltpu.VMEM((ROWS, COLS + 2 * WIDE), F32),
            pltpu.VMEM((WIDE, COLS), F32),
            pltpu.VMEM((WIDE, COLS), F32),
            pltpu.VMEM((WIDE, WIDE), F32),
            pltpu.VMEM((2, WIDE, WIDE), BF16),
            pltpu.VMEM((2, WIDE, WIDE), BF16),
            dma((chunks,)), dma((chunks,)),
            dma((16,)), dma((16,)), dma((8,)), dma((8,)), dma((16,)), dma((16,)), dma((16,)), dma((16,)),
        ],
        compiler_params=pltpu.CompilerParams(
            collective_id=0, has_side_effects=True, vmem_limit_bytes=56 * 1024 * 1024
        ),
        name="reduced_operators",
    )(
        order, diagonal, node_scale.reshape(nodes // 128, 128),
        jnp.transpose(panel_inverse, (1, 0, 2)), codes, basis,
    )


def solution(mesh):
    placed = (P("node", "tm"), P("node"), P("node", None), P(), P(), P())
    return jax.shard_map(
        per_device, mesh=mesh, in_specs=placed, out_specs=P("node", "tm"), check_vma=False
    )
```

```python
import jax
import jax.numpy as jnp
from jax import lax
from jax.experimental import pallas as pl
from jax.experimental.pallas import tpu as pltpu
from jax.sharding import PartitionSpec as P

MESH = pl.DeviceIdType.MESH
F32, BF16 = jnp.float32, jnp.bfloat16
ROWS = 528
COLS = 640
WIDE = 384
TALL = 272
COL_AT, FIRST_AT, SECOND_AT = COLS, 2 * COLS, 2 * COLS + WIDE
ALL = 2 * COLS + 2 * WIDE


def nt(left, right):
    return lax.dot_general(left, right, (((1,), (1,)), ((), ())), preferred_element_type=F32)


def nn(left, right):
    return lax.dot_general(left, right, (((1,), (0,)), ((), ())), preferred_element_type=F32)


def halves(values):
    high = values.astype(BF16)
    return high, (values - high.astype(F32)).astype(BF16)


def thrice(dot, left, right):
    return dot(left[0], right[0]) + dot(left[0], right[1]) + dot(left[1], right[0])


def kernel(
    order_hbm, regular_hbm, scale_hbm, panel_hbm, codes_hbm, basis_hbm, left_ref, up_ref, out_ref,
    codes_buf, basis_buf, scale_buf, order_buf, regular_buf, panel_buf, lines, order, regular,
    partial, slots, table, lead, trail, constant, feats,
    row_acc, up_acc, cross_acc, inv_high, inv_low,
    code_sem, basis_sem, small_sem, rs_send, rs_recv, one_send, one_recv, two_send, two_recv, sib_send, sib_recv,
):
    node, tm = lax.axis_index("node"), lax.axis_index("tm")
    x, z_hi = node // 4, node % 4
    z_lo, y, core = tm // 8, (tm // 2) % 4, tm % 2
    z = z_hi * 2 + z_lo
    inner, outer = y + core * (x - y), x + core * (y - x)
    modes = basis_buf.shape[1]
    width = panel_hbm.shape[0]
    size = out_ref.shape[0]

    def place(at_inner, at_outer, at_z, at_core):
        at_x = at_outer + core * (at_inner - at_outer)
        at_y = at_inner + core * (at_outer - at_inner)
        return (at_x * 4 + at_z // 2, (at_z % 2) * 8 + at_y * 2 + at_core)

    def node_peer(step):
        return ((node + step) % 16, tm)

    def one_peer(step):
        return place((inner + step // 8) % 4, outer, (z + step % 8) % 8, core)

    def two_peer(step):
        return place(inner, (outer + step) % 4, z, core)

    sibling = place(inner, outer, z, 1 - core)

    def rs_copy(step):
        peer = node_peer(step)
        return pltpu.make_async_remote_copy(
            src_ref=partial.at[peer[0]], dst_ref=slots.at[step],
            send_sem=rs_send.at[step], recv_sem=rs_recv.at[step],
            device_id=peer, device_id_type=MESH,
        )

    def one_copy(step):
        piece = table.at[core, outer, pl.ds((inner * 8 + z) * 8, 8)]
        return pltpu.make_async_remote_copy(
            src_ref=piece, dst_ref=piece, send_sem=one_send.at[step], recv_sem=one_recv.at[step],
            device_id=one_peer(step), device_id_type=MESH,
        )

    def two_copy(step):
        return pltpu.make_async_remote_copy(
            src_ref=table.at[core, outer], dst_ref=table.at[core, outer],
            send_sem=two_send.at[step], recv_sem=two_recv.at[step],
            device_id=two_peer(step), device_id_type=MESH,
        )

    def sib_copy(step):
        at = (outer + 4 - step) % 4
        return pltpu.make_async_remote_copy(
            src_ref=table.at[core, at], dst_ref=table.at[core, at],
            send_sem=sib_send.at[step], recv_sem=sib_recv.at[step],
            device_id=sibling, device_id_type=MESH,
        )

    chunks = code_sem.shape[0]
    rows = codes_buf.shape[0] // chunks

    def fetch(chunk):
        part = pl.ds(chunk * rows, rows)
        return (
            pltpu.make_async_copy(codes_hbm.at[part], codes_buf.at[part], code_sem.at[chunk]),
            pltpu.make_async_copy(basis_hbm.at[part], basis_buf.at[part], basis_sem.at[chunk]),
        )

    scale_copy = pltpu.make_async_copy(scale_hbm, scale_buf, small_sem.at[0])
    others = [
        pltpu.make_async_copy(order_hbm, order_buf, small_sem.at[1]),
        pltpu.make_async_copy(regular_hbm, regular_buf, small_sem.at[2]),
        pltpu.make_async_copy(panel_hbm, panel_buf, small_sem.at[3]),
    ]
    scale_copy.start()
    for chunk in range(chunks):
        for copy in fetch(chunk):
            copy.start()
    for copy in others:
        copy.start()

    barrier = pltpu.get_barrier_semaphore()

    def greet(peer):
        pl.semaphore_signal(barrier, inc=1, device_id=peer, device_id_type=MESH)

    @pl.loop(1, 16)
    def _(step):
        greet(node_peer(step))

    @pl.loop(1, 32)
    def _(step):
        greet(one_peer(step))

    @pl.loop(1, 4)
    def _(step):
        greet(two_peer(step))

    greet(sibling)

    total = jnp.zeros((modes, codes_buf.shape[1]), F32)
    scale_copy.wait()
    for chunk in range(chunks):
        for copy in fetch(chunk):
            copy.wait()
        turned = []
        for piece in range(rows // 128):
            row = chunk * (rows // 128) + piece
            basis = basis_buf[pl.ds(row * 128, 128), :].astype(F32)
            turned.append((basis.T * scale_buf[row : row + 1, :]).astype(BF16))
        values = codes_buf[pl.ds(chunk * rows, rows), :].astype(F32).astype(BF16)
        total = total + nn(jnp.concatenate(turned, axis=1), values)
    partial[...] = total.T.reshape(partial.shape)

    pl.semaphore_wait(barrier, 50)

    @pl.loop(1, 16)
    def _(step):
        rs_copy(step).start()

    for copy in others:
        copy.wait()
    row_from, col_from = node * size, tm * size
    lane = lax.broadcasted_iota(jnp.int32, (8, 128), 1)
    line = lax.broadcasted_iota(jnp.int32, (8, 128), 0)

    def unfold(flat, to_float):
        full = flat.shape[0] // 128
        for at in range(full):
            lines[at : at + 1, :] = to_float(flat[at * 128 : (at + 1) * 128].reshape(1, 128))
        rest = flat.shape[0] - full * 128
        lines[full : full + 1, 0:rest] = to_float(flat[full * 128 :].reshape(1, rest))

    def cut(low, count, height, fill):
        near = lines[pl.ds(low // 128, 8), :]
        shift = low % 128
        near = pltpu.roll(near, (128 - shift) % 128, 1)
        far = pltpu.roll(near, 7, 0)
        taken = jnp.where(lane < 128 - shift, near, far)
        return jnp.where(line * 128 + lane < count, taken, fill)[0:height]

    lines[64:80, :] = jnp.zeros((16, 128), F32)
    unfold(order_buf, lambda v: v.astype(F32))
    order[0:5, :] = cut(row_from, size, 5, -1.0)
    order[5:10, :] = cut(col_from, size, 5, -1.0)
    order[10:13, :] = cut(0, width, 3, -1.0)
    order[13:16, :] = cut(width, width, 3, -1.0)
    unfold(regular_buf, lambda v: v)
    regular[0:5, :] = cut(col_from, size, 5, 0.0)
    regular[5:8, :] = cut(0, width, 3, 0.0)
    regular[8:11, :] = cut(width, width, 3, 0.0)

    mode = lax.broadcasted_iota(jnp.int32, (128, 128), 1)
    start = mode * (modes + 1) - mode * (mode - 1) // 2

    @pl.loop(0, ALL // 128)
    def _(at):
        chosen = jnp.broadcast_to(order[pl.ds(at, 1), :], (128, 128)).T.astype(jnp.int32)
        among = jnp.logical_and(chosen >= start, chosen < start + (modes + 1 - mode))
        shift = jnp.sum(jnp.where(among, (mode - start).astype(F32), 0.0), axis=1, keepdims=True)
        trailing = chosen + jnp.broadcast_to(shift, (128, 128)).astype(jnp.int32)
        part = pl.ds(at * 128, 128)
        among = jnp.where(among, 1.0, 0.0).astype(BF16)
        lead[part, 0:128] = among
        lead[part, 128:256] = among
        same = jnp.where(trailing == mode, 1.0, 0.0).astype(BF16)
        trail[part, 0:128] = same
        trail[part, 128:256] = same
        constant[part, :] = jnp.where(trailing == modes, 1.0, 0.0)

    snapshots = 8 * table.shape[2]

    def diagonal(row_at, col_at, height, at):
        row = lax.broadcasted_iota(jnp.int32, (height, 128), 0) + row_at
        col = lax.broadcasted_iota(jnp.int32, (height, 128), 1) + col_at
        return jnp.where(row == col, regular[at : at + 1, :] * snapshots, 0.0)

    for at in range(11):
        part = slice(at * 128, at * 128 + 128)
        begin = col_from + at * 128 if at < 5 else (at - 5) * 128 if at < 8 else width + (at - 8) * 128
        row_acc[:, part] = diagonal(row_from, begin, ROWS, at)
        if at < 5:
            up_acc[0:WIDE, part] = diagonal(0, begin, WIDE, at)
            up_acc[WIDE:, part] = diagonal(width, begin, WIDE, at)
    cross_acc[...] = jnp.zeros_like(cross_acc)
    feats[...] = jnp.zeros_like(feats)
    inv_high[...] = jnp.zeros_like(inv_high)
    inv_low[...] = jnp.zeros_like(inv_low)
    for panel in range(2):
        high, low = halves(panel_buf[:, panel, :])
        inv_high[panel, 0:width, 0:width] = high
        inv_low[panel, 0:width, 0:width] = low

    @pl.loop(1, 16)
    def _(step):
        rs_copy(step).wait_recv()

    summed = partial[node]
    for step in range(1, 16):
        summed = summed + slots[step]
    table[core, outer, pl.ds((inner * 8 + z) * 8, 8), :] = summed

    @pl.loop(1, 32)
    def _(step):
        one_copy(step).start()

    @pl.loop(1, 32)
    def _(step):
        one_copy(step).wait_recv()

    for step in (1, 3, 2):
        two_copy(step).start()
    sib_copy(0).start()

    def own(step):
        return table[core, (outer + 4 - step) % 4]

    def other(step):
        return table[1 - core, (inner + 4 - step) % 4]

    def accumulate(first, second):
        values = jnp.concatenate([first, second], axis=0)
        pieces = jnp.concatenate(halves(values), axis=1)
        for low, count in ((0, ROWS), (COL_AT, ROWS), (FIRST_AT, TALL), (SECOND_AT, TALL)):
            part = slice(low, low + count)
            once = jnp.concatenate([constant[part, :]] * 4, axis=1)
            product = nt(lead[part, :], pieces) * (nt(trail[part, :], pieces) + once)
            feats[part, :] = product.astype(BF16)
        columns = feats[COL_AT:FIRST_AT, :]
        row_acc[...] += nt(feats[0:ROWS, :], feats[COL_AT:ALL, :])
        up_acc[0:TALL, :] += nt(feats[FIRST_AT : FIRST_AT + TALL, :], columns)
        later = feats[SECOND_AT : SECOND_AT + TALL, :]
        up_acc[WIDE : WIDE + TALL, :] += nt(later, columns)
        cross_acc[0:TALL, :] += nt(later, feats[FIRST_AT:SECOND_AT, :])

    sib_copy(0).wait_recv()
    accumulate(own(0), other(0))
    for step in (1, 3):
        two_copy(step).wait_recv()
        sib_copy(step).start()
    accumulate(own(1), own(3))
    two_copy(2).wait_recv()
    sib_copy(2).start()
    for step in (1, 3):
        sib_copy(step).wait_recv()
    accumulate(other(1), other(3))
    sib_copy(2).wait_recv()
    accumulate(own(2), other(2))

    share = 1.0 / snapshots
    first_inv = (inv_high[0], inv_low[0])
    second_inv = (inv_high[1], inv_low[1])
    cross = halves(cross_acc[...] * share)
    first_up = halves(up_acc[0:WIDE, :] * share)
    first_left = halves(row_acc[:, COLS : COLS + WIDE] * share)
    first_left = halves(thrice(nn, first_left, first_inv))
    second_left = row_acc[:, COLS + WIDE :] * share - thrice(nt, first_left, cross)
    second_left = thrice(nn, halves(second_left), second_inv)
    second_up = up_acc[WIDE:, :] * share - thrice(nn, halves(thrice(nn, cross, first_inv)), first_up)
    left_ref[:, 0:WIDE] = first_left[0][0:size]
    left_ref[:, WIDE:] = second_left[0:size].astype(BF16)
    up_ref[0:WIDE, :] = first_up[0][:, 0:size]
    up_ref[WIDE:, :] = second_up[:, 0:size].astype(BF16)
    out_ref[...] = row_acc[0:size, 0:size] * share

    @pl.loop(1, 16)
    def _(step):
        rs_copy(step).wait_send()

    @pl.loop(1, 32)
    def _(step):
        one_copy(step).wait_send()

    @pl.loop(1, 4)
    def _(step):
        two_copy(step).wait_send()

    @pl.loop(0, 4)
    def _(step):
        sib_copy(step).wait_send()


def per_device(codes, node_scale, basis, regular, feature_order, panel_inverse):
    nodes, snaps = codes.shape
    modes = basis.shape[1]
    size = regular.shape[0] // lax.axis_size("node")
    panels, width, _ = panel_inverse.shape
    chunks = 8
    dma = pltpu.SemaphoreType.DMA
    vmem = pl.BlockSpec(memory_space=pltpu.VMEM)
    hbm = pl.BlockSpec(memory_space=pltpu.HBM)
    left, up, matrix = pl.pallas_call(
        kernel,
        out_shape=(
            jax.ShapeDtypeStruct((size, 2 * WIDE), BF16),
            jax.ShapeDtypeStruct((2 * WIDE, size), BF16),
            jax.ShapeDtypeStruct((size, size), F32),
        ),
        in_specs=[hbm] * 6,
        out_specs=(vmem, vmem, vmem),
        scratch_shapes=[
            pltpu.VMEM((nodes, snaps), jnp.int32),
            pltpu.VMEM((nodes, modes), BF16),
            pltpu.VMEM((nodes // 128, 128), F32),
            pltpu.VMEM(feature_order.shape, jnp.int32),
            pltpu.VMEM(regular.shape, F32),
            pltpu.VMEM((width, panels, width), F32),
            pltpu.VMEM((80, 128), F32),
            pltpu.VMEM((16, 128), F32),
            pltpu.VMEM((16, 128), F32),
            pltpu.VMEM((16, 8, modes), F32),
            pltpu.VMEM((16, 8, modes), F32),
            pltpu.VMEM((2, 4, 256, modes), F32),
            pltpu.VMEM((ALL, 2 * modes), BF16),
            pltpu.VMEM((ALL, 2 * modes), BF16),
            pltpu.VMEM((ALL, 128), F32),
            pltpu.VMEM((ALL, 512), BF16),
            pltpu.VMEM((ROWS, COLS + 2 * WIDE), F32),
            pltpu.VMEM((2 * WIDE, COLS), F32),
            pltpu.VMEM((WIDE, WIDE), F32),
            pltpu.VMEM((2, WIDE, WIDE), BF16),
            pltpu.VMEM((2, WIDE, WIDE), BF16),
            dma((chunks,)), dma((chunks,)), dma((4,)),
            dma((16,)), dma((16,)), dma((32,)), dma((32,)), dma((4,)), dma((4,)), dma((4,)), dma((4,)),
        ],
        compiler_params=pltpu.CompilerParams(
            collective_id=0, has_side_effects=True, vmem_limit_bytes=40 * 1024 * 1024
        ),
        name="reduced_operators",
    )(*(
        pltpu.with_memory_space_constraint(each, pltpu.HBM)
        for each in (
            feature_order, regular, node_scale.reshape(nodes // 128, 128),
            jnp.transpose(panel_inverse, (1, 0, 2)), codes, basis,
        )
    ))
    return matrix - nn(left, up)


def solution(mesh):
    placed = (P("node", "tm"), P("node"), P("node", None), P(), P(), P())
    return jax.shard_map(
        per_device, mesh=mesh, in_specs=placed, out_specs=P("node", "tm"), check_vma=False
    )
```

```python
import jax
import jax.numpy as jnp
from jax import lax
from jax.experimental import pallas as pl
from jax.experimental.pallas import tpu as pltpu
from jax.sharding import PartitionSpec as P

MESH = pl.DeviceIdType.MESH
F32, BF16 = jnp.float32, jnp.bfloat16
ROWS = 528
COLS = 640
WIDE = 384
TALL = 272
COL_AT, FIRST_AT, SECOND_AT = COLS, 2 * COLS, 2 * COLS + WIDE
ALL = 2 * COLS + 2 * WIDE


def nt(left, right):
    return lax.dot_general(left, right, (((1,), (1,)), ((), ())), preferred_element_type=F32)


def nn(left, right):
    return lax.dot_general(left, right, (((1,), (0,)), ((), ())), preferred_element_type=F32)


def halves(values):
    high = values.astype(BF16)
    return high, (values - high.astype(F32)).astype(BF16)


def thrice(dot, left, right):
    return dot(left[0], right[0]) + dot(left[0], right[1]) + dot(left[1], right[0])


def kernel(
    order_hbm, regular_hbm, scale_hbm, panel_hbm, codes_hbm, basis_hbm, left_ref, up_ref, out_ref,
    codes_buf, basis_buf, scale_buf, order_buf, regular_buf, panel_buf, lines, order, regular,
    partial, slots, table, lead, trail, constant, feats,
    row_acc, up_acc, cross_acc, inv_high, inv_low,
    code_sem, basis_sem, small_sem, rs_send, rs_recv, z_send, z_recv, xy_send, xy_recv, sib_send, sib_recv,
):
    node, tm = lax.axis_index("node"), lax.axis_index("tm")
    x, z_hi = node // 4, node % 4
    z_lo, y, core = tm // 8, (tm // 2) % 4, tm % 2
    z = z_hi * 2 + z_lo
    modes = basis_buf.shape[1]
    width = panel_hbm.shape[0]
    size = out_ref.shape[0]

    chip = x * 4 + y

    def place(at_x, at_y, at_z, at_core):
        return (at_x * 4 + at_z // 2, (at_z % 2) * 8 + at_y * 2 + at_core)

    def node_peer(step):
        return ((node + step) % 16, tm)

    def z_peer(step):
        return place(x, y, (z + step) % 8, core)

    def xy_peer(step):
        return place((x + step // 4) % 4, (y + step % 4) % 4, z, core)

    def chip_from(step):
        return ((x + 4 - step // 4) % 4) * 4 + (y + 4 - step % 4) % 4

    sibling = place(x, y, z, 1 - core)

    def rs_copy(step):
        peer = node_peer(step)
        return pltpu.make_async_remote_copy(
            src_ref=partial.at[peer[0]], dst_ref=slots.at[step],
            send_sem=rs_send.at[step], recv_sem=rs_recv.at[step],
            device_id=peer, device_id_type=MESH,
        )

    def z_copy(step):
        piece = table.at[core, chip, pl.ds(z * 8, 8)]
        return pltpu.make_async_remote_copy(
            src_ref=piece, dst_ref=piece, send_sem=z_send.at[step], recv_sem=z_recv.at[step],
            device_id=z_peer(step), device_id_type=MESH,
        )

    def xy_copy(step):
        block = table.at[core, chip]
        return pltpu.make_async_remote_copy(
            src_ref=block, dst_ref=block, send_sem=xy_send.at[step], recv_sem=xy_recv.at[step],
            device_id=xy_peer(step), device_id_type=MESH,
        )

    def sib_copy(step):
        block = table.at[core, chip_from(step)]
        return pltpu.make_async_remote_copy(
            src_ref=block, dst_ref=block, send_sem=sib_send.at[step], recv_sem=sib_recv.at[step],
            device_id=sibling, device_id_type=MESH,
        )

    chunks = code_sem.shape[0]
    rows = codes_buf.shape[0] // chunks

    def fetch(chunk):
        part = pl.ds(chunk * rows, rows)
        return (
            pltpu.make_async_copy(codes_hbm.at[part], codes_buf.at[part], code_sem.at[chunk]),
            pltpu.make_async_copy(basis_hbm.at[part], basis_buf.at[part], basis_sem.at[chunk]),
        )

    scale_copy = pltpu.make_async_copy(scale_hbm, scale_buf, small_sem.at[0])
    others = [
        pltpu.make_async_copy(order_hbm, order_buf, small_sem.at[1]),
        pltpu.make_async_copy(regular_hbm, regular_buf, small_sem.at[2]),
        pltpu.make_async_copy(panel_hbm, panel_buf, small_sem.at[3]),
    ]
    scale_copy.start()
    for copy in fetch(0):
        copy.start()

    barrier = pltpu.get_barrier_semaphore()

    def greet(peer):
        pl.semaphore_signal(barrier, inc=1, device_id=peer, device_id_type=MESH)

    @pl.loop(1, 16)
    def _(step):
        greet(node_peer(step))

    for chunk in range(1, chunks):
        for copy in fetch(chunk):
            copy.start()

    @pl.loop(1, 16)
    def _(step):
        greet(xy_peer(step))

    @pl.loop(1, 8)
    def _(step):
        greet(z_peer(step))

    greet(sibling)
    for copy in others:
        copy.start()

    total = jnp.zeros((modes, codes_buf.shape[1]), F32)
    scale_copy.wait()
    for chunk in range(chunks):
        for copy in fetch(chunk):
            copy.wait()
        turned = []
        for piece in range(rows // 128):
            row = chunk * (rows // 128) + piece
            basis = basis_buf[pl.ds(row * 128, 128), :].T.astype(F32)
            turned.append((basis * scale_buf[row : row + 1, :]).astype(BF16))
        values = codes_buf[pl.ds(chunk * rows, rows), :].astype(F32).astype(BF16)
        total = total + nn(jnp.concatenate(turned, axis=1), values)
    partial[...] = total.T.reshape(partial.shape)

    pl.semaphore_wait(barrier, 38)

    @pl.loop(1, 16)
    def _(step):
        rs_copy(step).start()

    for copy in others:
        copy.wait()
    row_from, col_from = node * size, tm * size
    lane = lax.broadcasted_iota(jnp.int32, (8, 128), 1)
    line = lax.broadcasted_iota(jnp.int32, (8, 128), 0)

    def unfold(flat, to_float):
        full = flat.shape[0] // 128
        for at in range(full):
            lines[at : at + 1, :] = to_float(flat[at * 128 : (at + 1) * 128].reshape(1, 128))
        rest = flat.shape[0] - full * 128
        lines[full : full + 1, 0:rest] = to_float(flat[full * 128 :].reshape(1, rest))

    def cut(low, count, height, fill):
        near = lines[pl.ds(low // 128, 8), :]
        shift = low % 128
        near = pltpu.roll(near, (128 - shift) % 128, 1)
        far = pltpu.roll(near, 7, 0)
        taken = jnp.where(lane < 128 - shift, near, far)
        return jnp.where(line * 128 + lane < count, taken, fill)[0:height]

    lines[64:80, :] = jnp.zeros((16, 128), F32)
    unfold(order_buf, lambda v: v.astype(F32))
    order[0:5, :] = cut(row_from, size, 5, -1.0)
    order[5:10, :] = cut(col_from, size, 5, -1.0)
    order[10:13, :] = cut(0, width, 3, -1.0)
    order[13:16, :] = cut(width, width, 3, -1.0)
    unfold(regular_buf, lambda v: v)
    regular[0:5, :] = cut(col_from, size, 5, 0.0)
    regular[5:8, :] = cut(0, width, 3, 0.0)
    regular[8:11, :] = cut(width, width, 3, 0.0)

    mode = lax.broadcasted_iota(jnp.int32, (128, 128), 1)
    start = mode * (modes + 1) - mode * (mode - 1) // 2

    @pl.loop(0, ALL // 128)
    def _(at):
        chosen = jnp.broadcast_to(order[pl.ds(at, 1), :], (128, 128)).T.astype(jnp.int32)
        among = jnp.logical_and(chosen >= start, chosen < start + (modes + 1 - mode))
        shift = jnp.sum(jnp.where(among, (mode - start).astype(F32), 0.0), axis=1, keepdims=True)
        trailing = chosen + jnp.broadcast_to(shift, (128, 128)).astype(jnp.int32)
        part = pl.ds(at * 128, 128)
        among = jnp.where(among, 1.0, 0.0).astype(BF16)
        lead[part, 0:128] = among
        lead[part, 128:256] = among
        same = jnp.where(trailing == mode, 1.0, 0.0).astype(BF16)
        trail[part, 0:128] = same
        trail[part, 128:256] = same
        constant[part, :] = jnp.where(trailing == modes, 1.0, 0.0)

    snapshots = 32 * table.shape[2]

    def diagonal(row_at, col_at, height, at):
        row = lax.broadcasted_iota(jnp.int32, (height, 128), 0) + row_at
        col = lax.broadcasted_iota(jnp.int32, (height, 128), 1) + col_at
        return jnp.where(row == col, regular[at : at + 1, :] * snapshots, 0.0)

    for at in range(11):
        part = slice(at * 128, at * 128 + 128)
        begin = col_from + at * 128 if at < 5 else (at - 5) * 128 if at < 8 else width + (at - 8) * 128
        row_acc[:, part] = diagonal(row_from, begin, ROWS, at)
        if at < 5:
            up_acc[0:WIDE, part] = diagonal(0, begin, WIDE, at)
            up_acc[WIDE:, part] = diagonal(width, begin, WIDE, at)
    cross_acc[...] = jnp.zeros_like(cross_acc)
    feats[...] = jnp.zeros_like(feats)
    inv_high[...] = jnp.zeros_like(inv_high)
    inv_low[...] = jnp.zeros_like(inv_low)
    up_ref[WIDE + TALL :, :] = jnp.zeros((WIDE - TALL, size), BF16)
    for panel in range(2):
        high, low = halves(panel_buf[:, panel, :])
        inv_high[panel, 0:width, 0:width] = high
        inv_low[panel, 0:width, 0:width] = low

    @pl.loop(1, 16)
    def _(step):
        rs_copy(step).wait_recv()

    summed = partial[node]
    for step in range(1, 16):
        summed = summed + slots[step]
    table[core, chip, pl.ds(z * 8, 8), :] = summed

    @pl.loop(1, 8)
    def _(step):
        z_copy(step).start()

    @pl.loop(1, 8)
    def _(step):
        z_copy(step).wait_recv()

    batches = ((0, 4, 12, 1), (3, 8, 2, 5), (15, 7, 13, 9), (11, 6, 14, 10))
    for batch in batches:
        for step in batch:
            if step:
                xy_copy(step).start()

    def own(batch):
        return [table[core, chip_from(step)] for step in batch]

    def other(batch):
        return [table[1 - core, chip_from(step)] for step in batch]

    def take(batch):
        for step in batch:
            if step:
                xy_copy(step).wait_recv()
            sib_copy(step).start()

    def await_other(batch):
        for step in batch:
            sib_copy(step).wait_recv()

    def accumulate(blocks):
        values = jnp.concatenate(blocks, axis=0)
        snaps = values.shape[0]
        pieces = jnp.concatenate(halves(values), axis=1)
        for low, count in ((0, ROWS), (COL_AT, ROWS), (FIRST_AT, TALL), (SECOND_AT, TALL)):
            part = slice(low, low + count)
            once = jnp.concatenate([constant[part, :]] * (snaps // 128), axis=1)
            product = nt(lead[part, :], pieces) * (nt(trail[part, :], pieces) + once)
            feats[part, 0:snaps] = product.astype(BF16)
        columns = feats[COL_AT:FIRST_AT, 0:snaps]
        row_acc[...] += nt(feats[0:ROWS, 0:snaps], feats[COL_AT:ALL, 0:snaps])
        up_acc[0:TALL, :] += nt(feats[FIRST_AT : FIRST_AT + TALL, 0:snaps], columns)
        later = feats[SECOND_AT : SECOND_AT + TALL, 0:snaps]
        up_acc[WIDE : WIDE + TALL, :] += nt(later, columns)
        cross_acc[0:TALL, :] += nt(later, feats[FIRST_AT:SECOND_AT, 0:snaps])

    take(batches[0])
    accumulate(own(batches[0]))
    take(batches[1])
    accumulate(own(batches[1]))
    take(batches[2])
    await_other(batches[0])
    accumulate(own(batches[2]) + other(batches[0]))
    take(batches[3])
    await_other(batches[1])
    accumulate(own(batches[3]) + other(batches[1]))
    await_other(batches[2])
    await_other(batches[3])
    accumulate(other(batches[2]) + other(batches[3]))

    share = 1.0 / snapshots
    first_inv = (inv_high[0], inv_low[0])
    second_inv = (inv_high[1], inv_low[1])
    cross = halves(cross_acc[...] * share)
    first_up = (up_acc[0:WIDE, :] * share).astype(BF16)
    first_left = halves(row_acc[:, COLS : COLS + WIDE] * share)
    first_left = thrice(nn, first_left, first_inv).astype(BF16)
    short = (cross[0][0:TALL], cross[1][0:TALL])
    across = thrice(nn, short, first_inv).astype(BF16)
    second_left = row_acc[:, COLS + WIDE :] * share - nt(first_left, cross[0])
    second_left = thrice(nn, halves(second_left), second_inv)
    second_up = up_acc[WIDE : WIDE + TALL, :] * share - nn(across, first_up)
    left_ref[:, 0:WIDE] = first_left[0:size]
    left_ref[:, WIDE:] = second_left[0:size].astype(BF16)
    up_ref[0:WIDE, :] = first_up[:, 0:size]
    up_ref[WIDE : WIDE + TALL, :] = second_up[:, 0:size].astype(BF16)
    out_ref[...] = row_acc[0:size, 0:size] * share

    @pl.loop(1, 16)
    def _(step):
        rs_copy(step).wait_send()
        xy_copy(step).wait_send()

    @pl.loop(1, 8)
    def _(step):
        z_copy(step).wait_send()

    @pl.loop(0, 16)
    def _(step):
        sib_copy(step).wait_send()


def per_device(codes, node_scale, basis, regular, feature_order, panel_inverse):
    nodes, snaps = codes.shape
    modes = basis.shape[1]
    size = regular.shape[0] // lax.axis_size("node")
    panels, width, _ = panel_inverse.shape
    chunks = 4
    dma = pltpu.SemaphoreType.DMA
    vmem = pl.BlockSpec(memory_space=pltpu.VMEM)
    hbm = pl.BlockSpec(memory_space=pltpu.HBM)
    left, up, matrix = pl.pallas_call(
        kernel,
        out_shape=(
            jax.ShapeDtypeStruct((size, 2 * WIDE), BF16),
            jax.ShapeDtypeStruct((2 * WIDE, size), BF16),
            jax.ShapeDtypeStruct((size, size), F32),
        ),
        in_specs=[hbm] * 6,
        out_specs=(vmem, vmem, vmem),
        scratch_shapes=[
            pltpu.VMEM((nodes, snaps), jnp.int32),
            pltpu.VMEM((nodes, modes), BF16),
            pltpu.VMEM((nodes // 128, 128), F32),
            pltpu.VMEM(feature_order.shape, jnp.int32),
            pltpu.VMEM(regular.shape, F32),
            pltpu.VMEM((width, panels, width), F32),
            pltpu.VMEM((80, 128), F32),
            pltpu.VMEM((16, 128), F32),
            pltpu.VMEM((16, 128), F32),
            pltpu.VMEM((16, 8, modes), F32),
            pltpu.VMEM((16, 8, modes), F32),
            pltpu.VMEM((2, 16, 64, modes), F32),
            pltpu.VMEM((ALL, 2 * modes), BF16),
            pltpu.VMEM((ALL, 2 * modes), BF16),
            pltpu.VMEM((ALL, 128), F32),
            pltpu.VMEM((ALL, 512), BF16),
            pltpu.VMEM((ROWS, COLS + 2 * WIDE), F32),
            pltpu.VMEM((2 * WIDE, COLS), F32),
            pltpu.VMEM((WIDE, WIDE), F32),
            pltpu.VMEM((2, WIDE, WIDE), BF16),
            pltpu.VMEM((2, WIDE, WIDE), BF16),
            dma((chunks,)), dma((chunks,)), dma((4,)),
            dma((16,)), dma((16,)), dma((8,)), dma((8,)), dma((16,)), dma((16,)), dma((16,)), dma((16,)),
        ],
        compiler_params=pltpu.CompilerParams(
            collective_id=0, has_side_effects=True, vmem_limit_bytes=40 * 1024 * 1024
        ),
        name="reduced_operators",
    )(*(
        pltpu.with_memory_space_constraint(each, pltpu.HBM)
        for each in (
            feature_order, regular, node_scale.reshape(nodes // 128, 128),
            jnp.transpose(panel_inverse, (1, 0, 2)), codes, basis,
        )
    ))
    return matrix - nn(left, up)


def solution(mesh):
    placed = (P("node", "tm"), P("node"), P("node", None), P(), P(), P())
    return jax.shard_map(
        per_device, mesh=mesh, in_specs=placed, out_specs=P("node", "tm"), check_vma=False
    )
```

```python
import jax
import jax.numpy as jnp
from jax import lax
from jax.experimental import pallas as pl
from jax.experimental.pallas import tpu as pltpu
from jax.sharding import PartitionSpec as P

MESH = pl.DeviceIdType.MESH
F32, BF16 = jnp.float32, jnp.bfloat16
ROWS = 528
COLS = 640
WIDE = 384
TALL = 272
COL_AT, PAN_AT, ALL = COLS, 2 * COLS, 3 * COLS
LATE = 256


def nt(left, right):
    return lax.dot_general(left, right, (((1,), (1,)), ((), ())), preferred_element_type=F32)


def nn(left, right):
    return lax.dot_general(left, right, (((1,), (0,)), ((), ())), preferred_element_type=F32)


def halves(values):
    high = values.astype(BF16)
    return high, (values - high.astype(F32)).astype(BF16)


def thrice(left, right):
    return nn(jnp.concatenate([left[0], left[0], left[1]], axis=1), right)


def kernel(
    order_hbm, regular_hbm, scale_hbm, panel_hbm, codes_hbm, basis_hbm, left_ref, up_ref, out_ref,
    codes_buf, basis_buf, scale_buf, order_buf, regular_buf, panel_buf, lines, order, regular,
    partial, slots, table, lead, trail, constant, feats,
    row_acc, up_acc, cross_acc, square, inverse,
    code_sem, basis_sem, small_sem, rs_send, rs_recv, z_send, z_recv, xy_send, xy_recv, sib_send, sib_recv,
):
    node, tm = lax.axis_index("node"), lax.axis_index("tm")
    x, z_hi = node // 4, node % 4
    z_lo, y, core = tm // 8, (tm // 2) % 4, tm % 2
    z = z_hi * 2 + z_lo
    modes = basis_buf.shape[1]
    width = panel_hbm.shape[0]
    size = out_ref.shape[0]

    chip = x * 4 + y

    def place(at_x, at_y, at_z, at_core):
        return (at_x * 4 + at_z // 2, (at_z % 2) * 8 + at_y * 2 + at_core)

    def node_peer(step):
        return ((node + step) % 16, tm)

    def z_peer(step):
        return place(x, y, (z + step) % 8, core)

    def xy_peer(step):
        return place((x + step // 4) % 4, (y + step % 4) % 4, z, core)

    def chip_from(step):
        return ((x + 4 - step // 4) % 4) * 4 + (y + 4 - step % 4) % 4

    sibling = place(x, y, z, 1 - core)

    def rs_copy(step):
        peer = node_peer(step)
        return pltpu.make_async_remote_copy(
            src_ref=partial.at[peer[0]], dst_ref=slots.at[step],
            send_sem=rs_send.at[step], recv_sem=rs_recv.at[step],
            device_id=peer, device_id_type=MESH,
        )

    def z_copy(step):
        piece = table.at[core, chip, pl.ds(z * 8, 8)]
        return pltpu.make_async_remote_copy(
            src_ref=piece, dst_ref=piece, send_sem=z_send.at[step], recv_sem=z_recv.at[step],
            device_id=z_peer(step), device_id_type=MESH,
        )

    def xy_copy(step):
        block = table.at[core, chip]
        return pltpu.make_async_remote_copy(
            src_ref=block, dst_ref=block, send_sem=xy_send.at[step], recv_sem=xy_recv.at[step],
            device_id=xy_peer(step), device_id_type=MESH,
        )

    def sib_copy(step):
        block = table.at[core, chip_from(step)]
        return pltpu.make_async_remote_copy(
            src_ref=block, dst_ref=block, send_sem=sib_send.at[step], recv_sem=sib_recv.at[step],
            device_id=sibling, device_id_type=MESH,
        )

    chunks = code_sem.shape[0]
    rows = codes_buf.shape[0] // chunks

    def fetch(chunk):
        part = pl.ds(chunk * rows, rows)
        return (
            pltpu.make_async_copy(codes_hbm.at[part], codes_buf.at[part], code_sem.at[chunk]),
            pltpu.make_async_copy(basis_hbm.at[part], basis_buf.at[part], basis_sem.at[chunk]),
        )

    scale_copy = pltpu.make_async_copy(scale_hbm, scale_buf, small_sem.at[0])
    others = [
        pltpu.make_async_copy(order_hbm, order_buf, small_sem.at[1]),
        pltpu.make_async_copy(regular_hbm, regular_buf, small_sem.at[2]),
        pltpu.make_async_copy(panel_hbm, panel_buf, small_sem.at[3]),
    ]
    scale_copy.start()
    for copy in fetch(0):
        copy.start()

    barrier = pltpu.get_barrier_semaphore()

    def greet(peer):
        pl.semaphore_signal(barrier, inc=1, device_id=peer, device_id_type=MESH)

    @pl.loop(1, 16)
    def _(step):
        greet(node_peer(step))

    for chunk in range(1, chunks):
        for copy in fetch(chunk):
            copy.start()

    @pl.loop(1, 16)
    def _(step):
        greet(xy_peer(step))

    @pl.loop(1, 8)
    def _(step):
        greet(z_peer(step))

    greet(sibling)
    for copy in others:
        copy.start()

    total = jnp.zeros((modes, codes_buf.shape[1]), F32)
    scale_copy.wait()
    for chunk in range(chunks):
        for copy in fetch(chunk):
            copy.wait()
        turned = []
        for piece in range(rows // 128):
            row = chunk * (rows // 128) + piece
            basis = basis_buf[pl.ds(row * 128, 128), :].T.astype(F32)
            turned.append((basis * scale_buf[row : row + 1, :]).astype(BF16))
        values = codes_buf[pl.ds(chunk * rows, rows), :].astype(F32).astype(BF16)
        total = total + nn(jnp.concatenate(turned, axis=1), values)
    partial[...] = total.T.reshape(partial.shape)

    pl.semaphore_wait(barrier, 38)

    @pl.loop(1, 16)
    def _(step):
        rs_copy(step).start()

    for copy in others:
        copy.wait()
    row_from, col_from = node * size, tm * size
    lane = lax.broadcasted_iota(jnp.int32, (8, 128), 1)
    line = lax.broadcasted_iota(jnp.int32, (8, 128), 0)

    def unfold(flat, to_float):
        full = flat.shape[0] // 128
        for at in range(full):
            lines[at : at + 1, :] = to_float(flat[at * 128 : (at + 1) * 128].reshape(1, 128))
        rest = flat.shape[0] - full * 128
        lines[full : full + 1, 0:rest] = to_float(flat[full * 128 :].reshape(1, rest))

    def cut(low, count, height, fill):
        near = lines[pl.ds(low // 128, 8), :]
        shift = low % 128
        near = pltpu.roll(near, (128 - shift) % 128, 1)
        far = pltpu.roll(near, 7, 0)
        taken = jnp.where(lane < 128 - shift, near, far)
        return jnp.where(line * 128 + lane < count, taken, fill)[0:height]

    lines[64:80, :] = jnp.zeros((16, 128), F32)
    unfold(order_buf, lambda v: v.astype(F32))
    order[0:5, :] = cut(row_from, size, 5, -1.0)
    order[5:10, :] = cut(col_from, size, 5, -1.0)
    order[10:15, :] = cut(0, 2 * width, 5, -1.0)
    unfold(regular_buf, lambda v: v)
    regular[0:5, :] = cut(col_from, size, 5, 0.0)
    regular[5:10, :] = cut(0, 2 * width, 5, 0.0)

    mode = lax.broadcasted_iota(jnp.int32, (128, 128), 1)
    start = mode * (modes + 1) - mode * (mode - 1) // 2

    @pl.loop(0, ALL // 128)
    def _(at):
        chosen = jnp.broadcast_to(order[pl.ds(at, 1), :], (128, 128)).T.astype(jnp.int32)
        among = jnp.logical_and(chosen >= start, chosen < start + (modes + 1 - mode))
        shift = jnp.sum(jnp.where(among, (mode - start).astype(F32), 0.0), axis=1, keepdims=True)
        trailing = chosen + jnp.broadcast_to(shift, (128, 128)).astype(jnp.int32)
        part = pl.ds(at * 128, 128)
        among = jnp.where(among, 1.0, 0.0).astype(BF16)
        lead[part, 0:128] = among
        lead[part, 128:256] = among
        same = jnp.where(trailing == mode, 1.0, 0.0).astype(BF16)
        trail[part, 0:128] = same
        trail[part, 128:256] = same
        constant[part, :] = jnp.where(trailing == modes, 1.0, 0.0)

    snapshots = 32 * table.shape[2]

    def diagonal(row_at, col_at, height, at):
        row = lax.broadcasted_iota(jnp.int32, (height, 128), 0) + row_at
        col = lax.broadcasted_iota(jnp.int32, (height, 128), 1) + col_at
        return jnp.where(row == col, regular[at : at + 1, :] * snapshots, 0.0)

    for at in range(10):
        part = slice(at * 128, at * 128 + 128)
        begin = col_from + at * 128 if at < 5 else (at - 5) * 128
        row_acc[:, part] = diagonal(row_from, begin, ROWS, at)
        if at < 5:
            up_acc[:, part] = diagonal(0, begin, ROWS, at)
    cross_acc[...] = jnp.zeros_like(cross_acc)
    feats[...] = jnp.zeros_like(feats)
    square[...] = jnp.zeros_like(square)
    early = width - LATE
    for panel in range(2):
        square[0:width, 0:width] = panel_buf[:, panel, :]
        placed = square[...]
        if panel:
            placed = pltpu.roll(pltpu.roll(placed, early, 0), early, 1)
        high, low = halves(placed)
        inverse[panel, 0:WIDE, :] = high
        inverse[panel, WIDE : 2 * WIDE, :] = low
        inverse[panel, 2 * WIDE :, :] = high
    up_ref[ROWS:, :] = jnp.zeros((COLS - ROWS, size), BF16)

    @pl.loop(1, 16)
    def _(step):
        rs_copy(step).wait_recv()

    summed = partial[node]
    for step in range(1, 16):
        summed = summed + slots[step]
    table[core, chip, pl.ds(z * 8, 8), :] = summed

    @pl.loop(1, 8)
    def _(step):
        z_copy(step).start()

    @pl.loop(1, 8)
    def _(step):
        z_copy(step).wait_recv()

    batches = ((0, 4, 12, 1), (3, 8, 2, 5), (15, 7, 13, 9), (11, 6, 14, 10))
    for batch in batches:
        for step in batch:
            if step:
                xy_copy(step).start()

    def own(batch):
        return [table[core, chip_from(step)] for step in batch]

    def other(batch):
        return [table[1 - core, chip_from(step)] for step in batch]

    def take(batch):
        for step in batch:
            if step:
                xy_copy(step).wait_recv()
            sib_copy(step).start()

    def await_other(batch):
        for step in batch:
            sib_copy(step).wait_recv()

    def accumulate(blocks):
        values = jnp.concatenate(blocks, axis=0)
        snaps = values.shape[0]
        pieces = jnp.concatenate(halves(values), axis=1)
        for low, count in ((0, ROWS), (COL_AT, ROWS), (PAN_AT, ROWS)):
            part = slice(low, low + count)
            once = jnp.concatenate([constant[part, :]] * (snaps // 128), axis=1)
            product = nt(lead[part, :], pieces) * (nt(trail[part, :], pieces) + once)
            feats[part, 0:snaps] = product.astype(BF16)
        row_acc[...] += nt(feats[0:ROWS, 0:snaps], feats[COL_AT:ALL, 0:snaps])
        up_acc[...] += nt(feats[PAN_AT : PAN_AT + ROWS, 0:snaps], feats[COL_AT:PAN_AT, 0:snaps])
        later = feats[PAN_AT + LATE : PAN_AT + ROWS, 0:snaps]
        cross_acc[0:TALL, :] += nt(later, feats[PAN_AT : PAN_AT + WIDE, 0:snaps])

    take(batches[0])
    accumulate(own(batches[0]))
    take(batches[1])
    accumulate(own(batches[1]))
    take(batches[2])
    await_other(batches[0])
    accumulate(own(batches[2]) + other(batches[0]))
    take(batches[3])
    await_other(batches[1])
    accumulate(own(batches[3]) + other(batches[1]))
    await_other(batches[2])
    await_other(batches[3])
    accumulate(other(batches[2]) + other(batches[3]))

    share = 1.0 / snapshots
    late = lax.broadcasted_iota(jnp.int32, (WIDE, WIDE), 0) >= early
    soon = lax.broadcasted_iota(jnp.int32, (WIDE, WIDE), 1) < width
    cross = halves(jnp.where(jnp.logical_and(late, soon), cross_acc[...] * share, 0.0))
    first_left = thrice(halves(row_acc[:, COLS : COLS + WIDE] * share), inverse[0])
    short = (cross[0][0:TALL], cross[1][0:TALL])
    across = thrice(short, inverse[0]).astype(BF16)
    second_left = row_acc[:, COLS + LATE :] * share - nt(first_left.astype(BF16), cross[0])
    second_left = thrice(halves(second_left), inverse[1])
    first_up = (up_acc[0:WIDE, :] * share).astype(BF16)
    second_up = up_acc[LATE:, :] * share - nn(across, first_up)
    left_ref[:, 0:LATE] = first_left[0:size, 0:LATE].astype(BF16)
    both = first_left[0:size, LATE:] + second_left[0:size, 0 : WIDE - LATE]
    left_ref[:, LATE:WIDE] = both.astype(BF16)
    left_ref[:, WIDE:] = second_left[0:size, WIDE - LATE :].astype(BF16)
    up_ref[0:LATE, :] = first_up[0:LATE, 0:size]
    up_ref[LATE:ROWS, :] = second_up[:, 0:size].astype(BF16)
    out_ref[...] = row_acc[0:size, 0:size] * share

    @pl.loop(1, 16)
    def _(step):
        rs_copy(step).wait_send()
        xy_copy(step).wait_send()

    @pl.loop(1, 8)
    def _(step):
        z_copy(step).wait_send()

    @pl.loop(0, 16)
    def _(step):
        sib_copy(step).wait_send()


def per_device(codes, node_scale, basis, regular, feature_order, panel_inverse):
    nodes, snaps = codes.shape
    modes = basis.shape[1]
    size = regular.shape[0] // lax.axis_size("node")
    panels, width, _ = panel_inverse.shape
    chunks = 4
    dma = pltpu.SemaphoreType.DMA
    vmem = pl.BlockSpec(memory_space=pltpu.VMEM)
    hbm = pl.BlockSpec(memory_space=pltpu.HBM)
    left, up, matrix = pl.pallas_call(
        kernel,
        out_shape=(
            jax.ShapeDtypeStruct((size, COLS), BF16),
            jax.ShapeDtypeStruct((COLS, size), BF16),
            jax.ShapeDtypeStruct((size, size), F32),
        ),
        in_specs=[hbm] * 6,
        out_specs=(vmem, vmem, vmem),
        scratch_shapes=[
            pltpu.VMEM((nodes, snaps), jnp.int32),
            pltpu.VMEM((nodes, modes), BF16),
            pltpu.VMEM((nodes // 128, 128), F32),
            pltpu.VMEM(feature_order.shape, jnp.int32),
            pltpu.VMEM(regular.shape, F32),
            pltpu.VMEM((width, panels, width), F32),
            pltpu.VMEM((80, 128), F32),
            pltpu.VMEM((16, 128), F32),
            pltpu.VMEM((16, 128), F32),
            pltpu.VMEM((16, 8, modes), F32),
            pltpu.VMEM((16, 8, modes), F32),
            pltpu.VMEM((2, 16, 64, modes), F32),
            pltpu.VMEM((ALL, 2 * modes), BF16),
            pltpu.VMEM((ALL, 2 * modes), BF16),
            pltpu.VMEM((ALL, 128), F32),
            pltpu.VMEM((ALL, 512), BF16),
            pltpu.VMEM((ROWS, 2 * COLS), F32),
            pltpu.VMEM((ROWS, COLS), F32),
            pltpu.VMEM((WIDE, WIDE), F32),
            pltpu.VMEM((WIDE, WIDE), F32),
            pltpu.VMEM((2, 3 * WIDE, WIDE), BF16),
            dma((chunks,)), dma((chunks,)), dma((4,)),
            dma((16,)), dma((16,)), dma((8,)), dma((8,)), dma((16,)), dma((16,)), dma((16,)), dma((16,)),
        ],
        compiler_params=pltpu.CompilerParams(
            collective_id=0, has_side_effects=True, vmem_limit_bytes=40 * 1024 * 1024
        ),
        name="reduced_operators",
    )(*(
        pltpu.with_memory_space_constraint(each, pltpu.HBM)
        for each in (
            feature_order, regular, node_scale.reshape(nodes // 128, 128),
            jnp.transpose(panel_inverse, (1, 0, 2)), codes, basis,
        )
    ))
    return matrix - nn(left, up)


def solution(mesh):
    placed = (P("node", "tm"), P("node"), P("node", None), P(), P(), P())
    return jax.shard_map(
        per_device, mesh=mesh, in_specs=placed, out_specs=P("node", "tm"), check_vma=False
    )
```

```python
import jax
import jax.numpy as jnp
from jax import lax
from jax.experimental import pallas as pl
from jax.experimental.pallas import tpu as pltpu
from jax.sharding import PartitionSpec as P

MESH = pl.DeviceIdType.MESH
F32, BF16 = jnp.float32, jnp.bfloat16
ROWS = 528
COLS = 640
WIDE = 384
TALL = 272
COL_AT, PAN_AT, ALL = COLS, 2 * COLS, 3 * COLS
LATE = 256


def nt(left, right):
    return lax.dot_general(left, right, (((1,), (1,)), ((), ())), preferred_element_type=F32)


def nn(left, right):
    return lax.dot_general(left, right, (((1,), (0,)), ((), ())), preferred_element_type=F32)


def halves(values):
    high = values.astype(BF16)
    return high, (values - high.astype(F32)).astype(BF16)


def thrice(left, right):
    return nn(jnp.concatenate([left[0], left[0], left[1]], axis=1), right)


def kernel(
    order_hbm, regular_hbm, scale_hbm, panel_hbm, codes_hbm, basis_hbm, left_ref, up_ref, out_ref,
    codes_buf, basis_buf, scale_buf, order_buf, regular_buf, panel_buf, lines, order, regular,
    partial, slots, table, lead, trail, constant, feats,
    row_acc, up_acc, cross_acc, square, inverse,
    code_sem, basis_sem, small_sem, rs_send, rs_recv, z_send, z_recv, xy_send, xy_recv, sib_send, sib_recv,
):
    node, tm = lax.axis_index("node"), lax.axis_index("tm")
    x, z_hi = node // 4, node % 4
    z_lo, y, core = tm // 8, (tm // 2) % 4, tm % 2
    z = z_hi * 2 + z_lo
    modes = basis_buf.shape[1]
    width = panel_hbm.shape[0]
    size = out_ref.shape[0]

    chip = x * 4 + y

    def place(at_x, at_y, at_z, at_core):
        return (at_x * 4 + at_z // 2, (at_z % 2) * 8 + at_y * 2 + at_core)

    def node_peer(step):
        return ((node + step) % 16, tm)

    def z_peer(step):
        return place(x, y, (z + step) % 8, core)

    def xy_peer(step):
        along, across = step // 4, step % 4
        at_x = x + along + core * (across - along)
        at_y = y + across + core * (along - across)
        return place(at_x % 4, at_y % 4, z, core)

    def chip_from(step, at_core):
        along, across = step // 4, step % 4
        from_x = x + 4 - along - at_core * (across - along)
        from_y = y + 4 - across - at_core * (along - across)
        return (from_x % 4) * 4 + from_y % 4

    sibling = place(x, y, z, 1 - core)

    def rs_copy(step):
        peer = node_peer(step)
        return pltpu.make_async_remote_copy(
            src_ref=partial.at[peer[0]], dst_ref=slots.at[step],
            send_sem=rs_send.at[step], recv_sem=rs_recv.at[step],
            device_id=peer, device_id_type=MESH,
        )

    def z_copy(step):
        piece = table.at[core, chip, pl.ds(z * 8, 8)]
        return pltpu.make_async_remote_copy(
            src_ref=piece, dst_ref=piece, send_sem=z_send.at[step], recv_sem=z_recv.at[step],
            device_id=z_peer(step), device_id_type=MESH,
        )

    def xy_copy(step):
        block = table.at[core, chip]
        return pltpu.make_async_remote_copy(
            src_ref=block, dst_ref=block, send_sem=xy_send.at[step], recv_sem=xy_recv.at[step],
            device_id=xy_peer(step), device_id_type=MESH,
        )

    def sib_copy(step):
        block = table.at[core, chip_from(step, core)]
        return pltpu.make_async_remote_copy(
            src_ref=block, dst_ref=block, send_sem=sib_send.at[step], recv_sem=sib_recv.at[step],
            device_id=sibling, device_id_type=MESH,
        )

    chunks = code_sem.shape[0]
    rows = codes_buf.shape[0] // chunks

    def fetch(chunk):
        part = pl.ds(chunk * rows, rows)
        return (
            pltpu.make_async_copy(codes_hbm.at[part], codes_buf.at[part], code_sem.at[chunk]),
            pltpu.make_async_copy(basis_hbm.at[part], basis_buf.at[part], basis_sem.at[chunk]),
        )

    scale_copy = pltpu.make_async_copy(scale_hbm, scale_buf, small_sem.at[0])
    others = [
        pltpu.make_async_copy(order_hbm, order_buf, small_sem.at[1]),
        pltpu.make_async_copy(regular_hbm, regular_buf, small_sem.at[2]),
        pltpu.make_async_copy(panel_hbm, panel_buf, small_sem.at[3]),
    ]
    barrier = pltpu.get_barrier_semaphore()

    def greet(peer):
        pl.semaphore_signal(barrier, inc=1, device_id=peer, device_id_type=MESH)

    @pl.loop(1, 16)
    def _(step):
        greet(node_peer(step))

    scale_copy.start()
    for copy in fetch(0):
        copy.start()
    for chunk in range(1, chunks):
        for copy in fetch(chunk):
            copy.start()

    @pl.loop(1, 16)
    def _(step):
        greet(xy_peer(step))

    @pl.loop(1, 8)
    def _(step):
        greet(z_peer(step))

    greet(sibling)
    for copy in others:
        copy.start()

    total = jnp.zeros((modes, codes_buf.shape[1]), F32)
    scale_copy.wait()
    for chunk in range(chunks):
        for copy in fetch(chunk):
            copy.wait()
        turned = []
        for piece in range(rows // 128):
            row = chunk * (rows // 128) + piece
            basis = basis_buf[pl.ds(row * 128, 128), :].T.astype(F32)
            turned.append((basis * scale_buf[row : row + 1, :]).astype(BF16))
        values = codes_buf[pl.ds(chunk * rows, rows), :].astype(F32).astype(BF16)
        total = total + nn(jnp.concatenate(turned, axis=1), values)
    partial[...] = total.T.reshape(partial.shape)

    pl.semaphore_wait(barrier, 38)

    @pl.loop(1, 16)
    def _(step):
        rs_copy(step).start()

    for copy in others:
        copy.wait()
    row_from, col_from = node * size, tm * size
    lane = lax.broadcasted_iota(jnp.int32, (8, 128), 1)
    line = lax.broadcasted_iota(jnp.int32, (8, 128), 0)

    def unfold(flat, to_float):
        full = flat.shape[0] // 128
        for at in range(full):
            lines[at : at + 1, :] = to_float(flat[at * 128 : (at + 1) * 128].reshape(1, 128))
        rest = flat.shape[0] - full * 128
        lines[full : full + 1, 0:rest] = to_float(flat[full * 128 :].reshape(1, rest))

    def cut(low, count, height, fill):
        near = lines[pl.ds(low // 128, 8), :]
        shift = low % 128
        near = pltpu.roll(near, (128 - shift) % 128, 1)
        far = pltpu.roll(near, 7, 0)
        taken = jnp.where(lane < 128 - shift, near, far)
        return jnp.where(line * 128 + lane < count, taken, fill)[0:height]

    lines[64:80, :] = jnp.zeros((16, 128), F32)
    unfold(order_buf, lambda v: v.astype(F32))
    order[0:5, :] = cut(row_from, size, 5, -1.0)
    order[5:10, :] = cut(col_from, size, 5, -1.0)
    order[10:15, :] = cut(0, 2 * width, 5, -1.0)
    unfold(regular_buf, lambda v: v)
    regular[0:5, :] = cut(col_from, size, 5, 0.0)
    regular[5:10, :] = cut(0, 2 * width, 5, 0.0)

    mode = lax.broadcasted_iota(jnp.int32, (128, 128), 1)
    start = mode * (modes + 1) - mode * (mode - 1) // 2

    @pl.loop(0, ALL // 128)
    def _(at):
        chosen = jnp.broadcast_to(order[pl.ds(at, 1), :], (128, 128)).T.astype(jnp.int32)
        among = jnp.logical_and(chosen >= start, chosen < start + (modes + 1 - mode))
        shift = jnp.sum(jnp.where(among, (mode - start).astype(F32), 0.0), axis=1, keepdims=True)
        trailing = chosen + jnp.broadcast_to(shift, (128, 128)).astype(jnp.int32)
        part = pl.ds(at * 128, 128)
        among = jnp.where(among, 1.0, 0.0).astype(BF16)
        lead[part, 0:128] = among
        lead[part, 128:256] = among
        same = jnp.where(trailing == mode, 1.0, 0.0).astype(BF16)
        trail[part, 0:128] = same
        trail[part, 128:256] = same
        constant[part, :] = jnp.where(trailing == modes, 1.0, 0.0)

    snapshots = 32 * table.shape[2]

    def diagonal(row_at, col_at, height, at):
        row = lax.broadcasted_iota(jnp.int32, (height, 128), 0) + row_at
        col = lax.broadcasted_iota(jnp.int32, (height, 128), 1) + col_at
        return jnp.where(row == col, regular[at : at + 1, :] * snapshots, 0.0)

    for at in range(10):
        part = slice(at * 128, at * 128 + 128)
        begin = col_from + at * 128 if at < 5 else (at - 5) * 128
        row_acc[:, part] = diagonal(row_from, begin, ROWS, at)
        if at < 5:
            up_acc[:, part] = diagonal(0, begin, ROWS, at)
    cross_acc[...] = jnp.zeros_like(cross_acc)
    feats[...] = jnp.zeros_like(feats)
    square[...] = jnp.zeros_like(square)
    early = width - LATE
    for panel in range(2):
        square[0:width, 0:width] = panel_buf[:, panel, :]
        placed = square[...]
        if panel:
            placed = pltpu.roll(pltpu.roll(placed, early, 0), early, 1)
        high, low = halves(placed)
        inverse[panel, 0:WIDE, :] = high
        inverse[panel, WIDE : 2 * WIDE, :] = low
        inverse[panel, 2 * WIDE :, :] = high
    up_ref[ROWS:, :] = jnp.zeros((COLS - ROWS, size), BF16)

    @pl.loop(1, 16)
    def _(step):
        rs_copy(step).wait_recv()

    summed = partial[node]
    for step in range(1, 16):
        summed = summed + slots[step]
    table[core, chip, pl.ds(z * 8, 8), :] = summed

    @pl.loop(1, 8)
    def _(step):
        z_copy(step).start()

    @pl.loop(1, 8)
    def _(step):
        z_copy(step).wait_recv()

    batches = ((0, 4, 12, 1), (3, 8, 2, 5), (15, 7, 13, 9), (11, 6, 14, 10))
    for batch in batches:
        for step in batch:
            if step:
                xy_copy(step).start()

    def own(batch):
        return [table[core, chip_from(step, core)] for step in batch]

    def other(batch):
        return [table[1 - core, chip_from(step, 1 - core)] for step in batch]

    def take(batch):
        for step in batch:
            if step:
                xy_copy(step).wait_recv()
            sib_copy(step).start()

    def await_other(batch):
        for step in batch:
            sib_copy(step).wait_recv()

    def accumulate(blocks):
        values = jnp.concatenate(blocks, axis=0)
        snaps = values.shape[0]
        pieces = jnp.concatenate(halves(values), axis=1)
        for low, count in ((0, ROWS), (COL_AT, ROWS), (PAN_AT, ROWS)):
            part = slice(low, low + count)
            once = jnp.concatenate([constant[part, :]] * (snaps // 128), axis=1)
            product = nt(lead[part, :], pieces) * (nt(trail[part, :], pieces) + once)
            feats[part, 0:snaps] = product.astype(BF16)
        row_acc[...] += nt(feats[0:ROWS, 0:snaps], feats[COL_AT:ALL, 0:snaps])
        up_acc[...] += nt(feats[PAN_AT : PAN_AT + ROWS, 0:snaps], feats[COL_AT:PAN_AT, 0:snaps])
        later = feats[PAN_AT + LATE : PAN_AT + ROWS, 0:snaps]
        cross_acc[0:TALL, :] += nt(later, feats[PAN_AT : PAN_AT + WIDE, 0:snaps])

    take(batches[0])
    accumulate(own(batches[0]))
    take(batches[1])
    accumulate(own(batches[1]))
    take(batches[2])
    await_other(batches[0])
    accumulate(own(batches[2]) + other(batches[0]))
    take(batches[3])
    await_other(batches[1])
    accumulate(own(batches[3]) + other(batches[1]))
    await_other(batches[2])
    await_other(batches[3])
    accumulate(other(batches[2]) + other(batches[3]))

    share = 1.0 / snapshots
    late = lax.broadcasted_iota(jnp.int32, (WIDE, WIDE), 0) >= early
    soon = lax.broadcasted_iota(jnp.int32, (WIDE, WIDE), 1) < width
    cross = halves(jnp.where(jnp.logical_and(late, soon), cross_acc[...] * share, 0.0))
    first_left = thrice(halves(row_acc[:, COLS : COLS + WIDE] * share), inverse[0])
    short = (cross[0][0:TALL], cross[1][0:TALL])
    across = thrice(short, inverse[0]).astype(BF16)
    second_left = row_acc[:, COLS + LATE :] * share - nt(first_left.astype(BF16), cross[0])
    second_left = thrice(halves(second_left), inverse[1])
    first_up = (up_acc[0:WIDE, :] * share).astype(BF16)
    second_up = up_acc[LATE:, :] * share - nn(across, first_up)
    left_ref[:, 0:LATE] = first_left[0:size, 0:LATE].astype(BF16)
    both = first_left[0:size, LATE:] + second_left[0:size, 0 : WIDE - LATE]
    left_ref[:, LATE:WIDE] = both.astype(BF16)
    left_ref[:, WIDE:] = second_left[0:size, WIDE - LATE :].astype(BF16)
    up_ref[0:LATE, :] = first_up[0:LATE, 0:size]
    up_ref[LATE:ROWS, :] = second_up[:, 0:size].astype(BF16)
    out_ref[...] = row_acc[0:size, 0:size] * share

    @pl.loop(1, 16)
    def _(step):
        rs_copy(step).wait_send()
        xy_copy(step).wait_send()

    @pl.loop(1, 8)
    def _(step):
        z_copy(step).wait_send()

    @pl.loop(0, 16)
    def _(step):
        sib_copy(step).wait_send()


def finish(left_ref, up_ref, matrix_ref, out_hbm, result, sem):
    size = result.shape[0]
    copies = []
    for at, low in enumerate(range(0, size, 176)):
        part = slice(low, min(low + 176, size))
        result[part, :] = matrix_ref[part, :] - nn(left_ref[part, :], up_ref[...])
        copy = pltpu.make_async_copy(result.at[part], out_hbm.at[part], sem.at[at])
        copy.start()
        copies.append(copy)
    for copy in copies:
        copy.wait()


def per_device(codes, node_scale, basis, regular, feature_order, panel_inverse):
    nodes, snaps = codes.shape
    modes = basis.shape[1]
    size = regular.shape[0] // lax.axis_size("node")
    panels, width, _ = panel_inverse.shape
    chunks = 4
    dma = pltpu.SemaphoreType.DMA
    vmem = pl.BlockSpec(memory_space=pltpu.VMEM)
    hbm = pl.BlockSpec(memory_space=pltpu.HBM)
    left, up, matrix = pl.pallas_call(
        kernel,
        out_shape=(
            jax.ShapeDtypeStruct((size, COLS), BF16),
            jax.ShapeDtypeStruct((COLS, size), BF16),
            jax.ShapeDtypeStruct((size, size), F32),
        ),
        in_specs=[hbm] * 6,
        out_specs=(vmem, vmem, vmem),
        scratch_shapes=[
            pltpu.VMEM((nodes, snaps), jnp.int32),
            pltpu.VMEM((nodes, modes), BF16),
            pltpu.VMEM((nodes // 128, 128), F32),
            pltpu.VMEM(feature_order.shape, jnp.int32),
            pltpu.VMEM(regular.shape, F32),
            pltpu.VMEM((width, panels, width), F32),
            pltpu.VMEM((80, 128), F32),
            pltpu.VMEM((16, 128), F32),
            pltpu.VMEM((16, 128), F32),
            pltpu.VMEM((16, 8, modes), F32),
            pltpu.VMEM((16, 8, modes), F32),
            pltpu.VMEM((2, 16, 64, modes), F32),
            pltpu.VMEM((ALL, 2 * modes), BF16),
            pltpu.VMEM((ALL, 2 * modes), BF16),
            pltpu.VMEM((ALL, 128), F32),
            pltpu.VMEM((ALL, 512), BF16),
            pltpu.VMEM((ROWS, 2 * COLS), F32),
            pltpu.VMEM((ROWS, COLS), F32),
            pltpu.VMEM((WIDE, WIDE), F32),
            pltpu.VMEM((WIDE, WIDE), F32),
            pltpu.VMEM((2, 3 * WIDE, WIDE), BF16),
            dma((chunks,)), dma((chunks,)), dma((4,)),
            dma((16,)), dma((16,)), dma((8,)), dma((8,)), dma((16,)), dma((16,)), dma((16,)), dma((16,)),
        ],
        compiler_params=pltpu.CompilerParams(
            collective_id=0, has_side_effects=True, vmem_limit_bytes=40 * 1024 * 1024
        ),
        name="reduced_operators",
    )(*(
        pltpu.with_memory_space_constraint(each, pltpu.HBM)
        for each in (
            feature_order, regular, node_scale.reshape(nodes // 128, 128),
            jnp.transpose(panel_inverse, (1, 0, 2)), codes, basis,
        )
    ))
    return pl.pallas_call(
        finish,
        out_shape=jax.ShapeDtypeStruct((size, size), F32),
        in_specs=[vmem, vmem, vmem],
        out_specs=hbm,
        scratch_shapes=[pltpu.VMEM((size, size), F32), dma((3,))],
        cost_estimate=pl.CostEstimate(
            flops=2 * size * size * COLS, bytes_accessed=4 * size * size, transcendentals=0
        ),
        compiler_params=pltpu.CompilerParams(vmem_limit_bytes=16 * 1024 * 1024),
        name="subtract_product",
    )(left, up, matrix)


def solution(mesh):
    placed = (P("node", "tm"), P("node"), P("node", None), P(), P(), P())
    return jax.shard_map(
        per_device, mesh=mesh, in_specs=placed, out_specs=P("node", "tm"), check_vma=False
    )
```
